512 devices in a mesh: lon: 32 (over z, core), lat: 16 (over y, x).
Axes of the slice: x: 4, y: 4, z: 16, core: 2. Of those that a mesh axis runs over, the one named last changes fastest.
Arguments:
- perturbations: float32 [12, 3, 256, 4096], P(None, None, 'lat', 'lon'), as said below
- base_wind: float32 [2, 256, 4096], P(None, 'lat', 'lon'), may hold values from -4 to 4
- base_height: float32 [256, 4096], P('lat', 'lon'), may hold values from 0.5 to 1.5
Outputs:
- fields: float32 [12, 3, 256, 4096], P(None, None, 'lat', 'lon')
- factor: float32 [12, 12], replicated
The draws below stay inside these ranges and needn't reach their ends.
Inputs may be any that keep to these rules, and one draw needn't show every extreme that they name: `perturbations`: finite real values.
All inputs are finite; a program needn't handle non-finite values.
Results may differ from the reference program's by a relative error of at most 0.00012.
Values sent between devices are 32-bit elements; how exact they have to be, the bound alone decides.
A program may use at most 64 MiB of HBM per device.

```python
import math
import jax
import jax.numpy as jnp
from jax import lax

MEMBERS = 12
VARS = 3
STEPS = 8
NLON = 4096
NLAT = 256


def draw_perturbations(key, part):
    keys = jax.random.split(key, 3)
    shape = (MEMBERS, 3, NLAT, NLON)
    values = jnp.clip(jax.random.normal(keys[0], shape, jnp.float32), -4.0, 4.0)
    cells = jnp.exp(math.log(10.0) * jax.random.uniform(keys[1], (1, 3, NLAT, NLON), jnp.float32))
    columns = jnp.exp(math.log(10.0) * jax.random.uniform(keys[2], (MEMBERS, 1, 1, 1), jnp.float32))
    rise_lat = 1.0 + jnp.arange(NLAT, dtype=jnp.float32) / NLAT
    rise_lon = 1.0 + jnp.arange(NLON, dtype=jnp.float32) / NLON
    rise = rise_lat[:, None] * rise_lon[None, :]
    return (values * cells * columns * rise).astype(jnp.float32)


def block_levels(own_key, dims, cuts, smallest, high):
    def one(dim, parts):
        steps = jax.random.uniform(jax.random.fold_in(jax.random.fold_in(own_key, 6), dim), (parts,), jnp.float32, smallest / len(cuts), high / len(cuts))
        return jnp.repeat(jnp.exp(steps), dims[dim] // parts).reshape((-1,) + (1,) * (len(dims) - dim - 1))

    gain = one(*cuts[0])
    for cut in cuts[1:]:
        gain = gain * one(*cut)
    return gain


def normal_values(key, shape, spread, bound, cuts=(), kind=jnp.bfloat16):
    level = block_levels(key, shape, cuts, -0.22, 0.18) if cuts else 1.0
    values = jax.random.normal(key, shape, jnp.float32) * spread * level
    return jnp.minimum(jnp.maximum(values, -bound), bound).astype(kind)


def setup_inputs(seed: int = 0) -> dict:
    streams_of = jax.random.split(jax.random.key(seed), 4)
    return {
        "perturbations": draw_perturbations(jax.random.fold_in(streams_of[3], 71), 0),
        "base_wind": normal_values(streams_of[1], (2, NLAT, NLON), 1.0, 4.0, ((1, 16), (2, 32)), jnp.float32),
        "base_height": jnp.clip(0.5 + 1.0 * jax.random.uniform(streams_of[2], (NLAT, NLON), jnp.float32) ** block_levels(streams_of[2], (NLAT, NLON), ((0, 16), (1, 32)), -0.2, 0.2), 0.5, 1.5),
    }


advect_rate = 0.1
turn_rate = 0.5
gravity_rate = 0.2
diffuse_rate = 0.12

def centre(array):
    return array[..., 1:-1, 1:-1]

def diff_lon(array):
    return 0.5 * (array[..., 1:-1, 2:] - array[..., 1:-1, :-2])

def diff_lat(array):
    return 0.5 * (array[..., 2:, 1:-1] - array[..., :-2, 1:-1])

def laplacian(array):
    return array[..., 2:, 1:-1] + array[..., :-2, 1:-1] + array[..., 1:-1, 2:] + array[..., 1:-1, :-2] - 4.0 * centre(array)

def advance(field, base, turning):
    wind_x = field[..., 0, :, :]
    wind_y = field[..., 1, :, :]
    height = field[..., 2, :, :]
    base_x = base[0]
    base_y = base[1]
    base_depth = base[2]
    mean_x = centre(base_x)
    mean_y = centre(base_y)
    inner_x = centre(wind_x)
    inner_y = centre(wind_y)
    new_x = inner_x - advect_rate * (mean_x * diff_lon(wind_x) + inner_x * diff_lon(base_x) + mean_y * diff_lat(wind_x) + inner_y * diff_lat(base_x)) + turn_rate * turning * inner_y - gravity_rate * diff_lon(height) + diffuse_rate * laplacian(wind_x)
    new_y = inner_y - advect_rate * (mean_x * diff_lon(wind_y) + inner_x * diff_lon(base_y) + mean_y * diff_lat(wind_y) + inner_y * diff_lat(base_y)) - turn_rate * turning * inner_x - gravity_rate * diff_lat(height) + diffuse_rate * laplacian(wind_y)
    new_height = centre(height) - advect_rate * (diff_lon(base_depth * wind_x + height * base_x) + diff_lat(base_depth * wind_y + height * base_y)) + diffuse_rate * laplacian(height)
    return jnp.stack([new_x, new_y, new_height], axis=-3)

def coriolis(start, rows, total):
    glob = (start + jnp.arange(rows, dtype=jnp.int32)).astype(jnp.float32)
    return jnp.sin(math.pi * ((glob + 0.5) / total - 0.5))[:, None]

def extend_grid(array, width):
    lead = [(0, 0)] * (array.ndim - 2)
    wrapped = jnp.pad(array, lead + [(0, 0), (width, width)], mode='wrap')
    return jnp.pad(wrapped, lead + [(width, width), (0, 0)])

def reference(perturbations, base_wind, base_height):
    base = jnp.concatenate([base_wind, base_height[None]], axis=0)
    base_ext = extend_grid(base, 1)
    turning = coriolis(0, NLAT, NLAT)

    def evolve(member):
        for step_index in range(STEPS):
            member = advance(extend_grid(member, 1), base_ext, turning)
        return member
    evolved = lax.map(evolve, perturbations)
    flattened = evolved.reshape(MEMBERS, -1)
    cell_count = float(VARS * NLAT * NLON)
    gram = jnp.dot(flattened, flattened.T, precision=lax.Precision.HIGHEST) / cell_count
    lower_factor = jnp.linalg.cholesky(gram)
    fields = jax.scipy.linalg.solve_triangular(lower_factor, flattened, lower=True)
    return (fields.reshape(perturbations.shape), lower_factor.T)
```

```python
import functools
import math

import jax
import jax.numpy as jnp
from jax import lax
from jax.experimental import pallas as pl
from jax.experimental.pallas import tpu as pltpu
from jax.sharding import PartitionSpec as P

MEMBERS = 12
STEPS = 8
GROUP = 4
GROUPS = MEMBERS // GROUP
WIDTH = 8
EDGE = 24
STRIP = 32

advect_rate = 0.1
turn_rate = 0.5
gravity_rate = 0.2
diffuse_rate = 0.12

HALF = 0.5 * advect_rate
KEEP = 1.0 - 4.0 * diffuse_rate
PULL = 0.5 * gravity_rate
COEFS = 13


def roll(value, shift):
    shift = shift % 128
    return value if shift == 0 else pltpu.roll(value, shift, 1)


def lanes_of(rows):
    return lax.broadcasted_iota(jnp.int32, (rows, 128), 1)


def rows_of(rows):
    return lax.broadcasted_iota(jnp.int32, (rows, 128), 0)


def slot_of(local, var):
    return WIDTH * (3 * local + var)


def kernel(
    n_lon,
    n_lat,
    x_hbm,
    wind_hbm,
    height_hbm,
    fields_ref,
    factor_ref,
    ext,
    send_low,
    send_high,
    from_west,
    from_east,
    flow,
    base,
    coef,
    evolved,
    table,
    row_out,
    plane_in,
    column_in,
    load_sem,
    lat_send,
    lat_recv,
    strip_send,
    strip_recv,
    plane_send,
    plane_recv,
    column_send,
    column_recv,
):
    lon = lax.axis_index("lon")
    lat = lax.axis_index("lat")
    level = lon // 2
    core = lon % 2
    n_level = n_lon // 2
    n_plane = 2 * n_lat
    me_plane = lat * 2 + core
    east = (lon + 1) % n_lon
    west = (lon + n_lon - 1) % n_lon
    has_south = lat > 0
    has_north = lat < n_lat - 1

    def device(lon_index, lat_index):
        return {"lon": lon_index, "lat": lat_index}

    loads = [
        pltpu.make_async_copy(x_hbm, ext.at[0:MEMBERS, :, 8:24], load_sem.at[0]),
        pltpu.make_async_copy(wind_hbm, ext.at[MEMBERS, 0:2, 8:24], load_sem.at[1]),
        pltpu.make_async_copy(height_hbm, ext.at[MEMBERS, 2, 8:24], load_sem.at[2]),
    ]
    for load in loads:
        load.start()

    def plane_peer(step):
        index = (me_plane + step) % n_plane
        return device(level * 2 + index % 2, index // 2)

    def column_peer(step):
        return device(((level + step) % n_level) * 2 + core, lat)

    barrier = pltpu.get_barrier_semaphore()
    across = jnp.where(core == 1, east, west)

    @pl.loop(1, n_plane)
    def _(step):
        pl.semaphore_signal(barrier, inc=1, device_id=plane_peer(step))

    @pl.loop(1, n_level)
    def _(step):
        pl.semaphore_signal(barrier, inc=1, device_id=column_peer(step))

    pl.semaphore_signal(barrier, inc=1, device_id=device(across, lat))

    @pl.when(has_south)
    def _():
        pl.semaphore_signal(barrier, inc=1, device_id=device(across, lat - 1))

    @pl.when(has_north)
    def _():
        pl.semaphore_signal(barrier, inc=1, device_id=device(across, lat + 1))

    def lat_copies(piece, north):
        rows = pl.ds(8, 8) if north else pl.ds(0, 8)
        place = pl.ds(0, 8) if north else pl.ds(24, 8)
        way = 0 if north else 1
        target = device(lon, lat + 1 if north else lat - 1)
        if piece == "wind":
            source, goal, sem = wind_hbm.at[:, rows], ext.at[MEMBERS, 0:2, place], GROUPS
        elif piece == "height":
            source, goal, sem = height_hbm.at[rows], ext.at[MEMBERS, 2, place], GROUPS + 1
        else:
            members = pl.ds(piece * GROUP, GROUP)
            source, goal, sem = x_hbm.at[members, :, rows], ext.at[members, :, place], piece
        return pltpu.make_async_remote_copy(
            src_ref=source,
            dst_ref=goal,
            send_sem=lat_send.at[way, sem],
            recv_sem=lat_recv.at[way, sem],
            device_id=target,
        )

    def strip_copy(to_east, shift):
        packed = send_high if to_east else send_low
        goal = from_west if to_east else from_east
        rows = {0: pl.ds(0, 16), 1: pl.ds(8, 8), -1: pl.ds(0, 8)}[shift]
        place = {0: pl.ds(8, 16), 1: pl.ds(0, 8), -1: pl.ds(24, 8)}[shift]
        sem = (0 if to_east else 3) + shift + 1
        return pltpu.make_async_remote_copy(
            src_ref=packed.at[:, rows],
            dst_ref=goal.at[:, place],
            send_sem=strip_send.at[sem],
            recv_sem=strip_recv.at[sem],
            device_id=device(east if to_east else west, lat + shift),
        )

    def when_sends(north, body):
        pl.when(has_north if north else has_south)(body)

    def when_receives(north, body):
        pl.when(has_south if north else has_north)(body)

    lane8 = lanes_of(8)

    for load in loads:
        load.wait()

    lane16 = lanes_of(16)

    @pl.loop(0, GROUPS)
    def _(group):
        low = jnp.zeros((16, 128), jnp.float32)
        high = jnp.zeros((16, 128), jnp.float32)
        for local in range(GROUP + 1):
            for var in range(3):
                value = ext[group * GROUP + local if local < GROUP else MEMBERS, var, pl.ds(8, 16)]
                slot = slot_of(local, var)
                inside = (lane16 >= slot) & (lane16 < slot + WIDTH)
                low = jnp.where(inside, roll(value, slot), low)
                high = jnp.where(inside, roll(value, slot - 120), high)
        send_low[group] = low
        send_high[group] = high

    pl.semaphore_wait(
        barrier,
        n_plane - 1 + n_level - 1 + 1 + has_south.astype(jnp.int32) + has_north.astype(jnp.int32),
    )

    for piece in ("wind", "height"):
        for north in (True, False):
            when_sends(north, lambda: lat_copies(piece, north).start())
    for to_east in (True, False):
        strip_copy(to_east, 0).start()
        pl.when(has_north)(lambda: strip_copy(to_east, 1).start())
        pl.when(has_south)(lambda: strip_copy(to_east, -1).start())
    for piece in range(GROUPS):
        for north in (True, False):
            when_sends(north, lambda: lat_copies(piece, north).start())

    evolved[MEMBERS * 48 :, :] = jnp.zeros((4 * 48, 128), jnp.float32)
    for parity in range(2):
        for slot in range(GROUP + 1):
            for var in range(3):
                flow[parity, slot, var, 0:8] = jnp.zeros((8, 128), jnp.float32)
                flow[parity, slot, var, 40:48] = jnp.zeros((8, 128), jnp.float32)
    for kind in range(2):
        for var in range(3):
            base[kind, var, 0:8] = jnp.zeros((8, 128), jnp.float32)
            base[kind, var, 40:48] = jnp.zeros((8, 128), jnp.float32)

    for piece in ("wind", "height"):
        for north in (True, False):
            when_receives(north, lambda: lat_copies(piece, north).wait_recv())
    for to_east in (True, False):
        strip_copy(to_east, 0).wait_recv()
        pl.when(has_south)(lambda: strip_copy(to_east, 1).wait_recv())
        pl.when(has_north)(lambda: strip_copy(to_east, -1).wait_recv())

    def present(tile, value):
        if tile == 0:
            return jnp.where(has_south, value, 0.0)
        if tile == 3:
            return jnp.where(has_north, value, 0.0)
        return value

    def shifted_main(group, member, local, var, tile):
        rows = pl.ds(8 * tile, 8)
        rim = roll(from_west[group, rows], -slot_of(local, var))
        return present(tile, jnp.where(lane8 < WIDTH, rim, roll(ext[member, var, rows], WIDTH)))

    def strip_part(total, group, member, local, var, place, tile):
        rows = pl.ds(8 * tile, 8)
        first = place * STRIP
        own = roll(ext[member, var, rows], first - (128 - EDGE))
        rim = roll(from_east[group, rows], first + EDGE - slot_of(local, var))
        total = jnp.where((lane8 >= first) & (lane8 < first + EDGE), own, total)
        return jnp.where((lane8 >= first + EDGE) & (lane8 < first + STRIP), rim, total)

    for var in range(3):
        for tile in range(4):
            rows = pl.ds(8 + 8 * tile, 8)
            base[0, var, rows] = shifted_main(0, MEMBERS, GROUP, var, tile)
            total = jnp.zeros((8, 128), jnp.float32)
            for place in range(4):
                total = strip_part(total, 0, MEMBERS, GROUP, var, place, tile)
            base[1, var, rows] = present(tile, total)
    for tile in range(4):
        place = (lat * 16 - 8 + 8 * tile + rows_of(8)).astype(jnp.float32)
        turning = jnp.sin(math.pi * ((place + 0.5) / (16 * n_lat) - 0.5))
        for kind in range(2):
            here, up, down = pl.ds(8 + 8 * tile, 8), pl.ds(9 + 8 * tile, 8), pl.ds(7 + 8 * tile, 8)
            mean_x = base[kind, 0, here]
            mean_y = base[kind, 1, here]
            depth = base[kind, 2, here]
            x_up, x_down = base[kind, 0, up], base[kind, 0, down]
            y_up, y_down = base[kind, 1, up], base[kind, 1, down]
            values = [
                diffuse_rate - HALF * mean_x,
                diffuse_rate + HALF * mean_x,
                diffuse_rate - HALF * mean_y,
                diffuse_rate + HALF * mean_y,
                KEEP - HALF * (roll(mean_x, -1) - roll(mean_x, 1)),
                turn_rate * turning - HALF * (x_up - x_down),
                KEEP - HALF * (y_up - y_down),
                -turn_rate * turning - HALF * (roll(mean_y, -1) - roll(mean_y, 1)),
                HALF * depth,
                diffuse_rate - HALF * y_up,
                diffuse_rate + HALF * y_down,
                HALF * base[kind, 2, up],
                HALF * base[kind, 2, down],
            ]
            for index, value in enumerate(values):
                coef[index, kind, pl.ds(8 * tile, 8)] = value

    def advance(source, target, tiles):
        for tile in tiles:
            here, up, down = pl.ds(8 + 8 * tile, 8), pl.ds(9 + 8 * tile, 8), pl.ds(7 + 8 * tile, 8)
            for kind, slots in ((0, range(GROUP)), (1, (GROUP,))):
                (e, w, n, s, keep_x, turn_x, keep_y, turn_y, deep, n_h, s_h, n_deep, s_deep) = [
                    coef[index, kind, pl.ds(8 * tile, 8)] for index in range(COEFS)
                ]
                for slot in slots:
                    u, u_n, u_s = (flow[source, slot, 0, r] for r in (here, up, down))
                    v, v_n, v_s = (flow[source, slot, 1, r] for r in (here, up, down))
                    h, h_n, h_s = (flow[source, slot, 2, r] for r in (here, up, down))
                    new_u = (
                        (keep_x * u + turn_x * v)
                        + (n * u_n + s * u_s)
                        + (e * roll(u, -1) + w * roll(u, 1))
                        - PULL * (roll(h, -1) - roll(h, 1))
                    )
                    new_v = (
                        (keep_y * v + turn_y * u)
                        + (n * v_n + s * v_s)
                        + (e * roll(v, -1) + w * roll(v, 1))
                        - PULL * (h_n - h_s)
                    )
                    carried = deep * u
                    new_h = (
                        KEEP * h
                        + (roll(e * h - carried, -1) + roll(w * h + carried, 1))
                        + (n_h * h_n + s_h * h_s)
                        - (n_deep * v_n - s_deep * v_s)
                    )
                    flow[target, slot, 0, here] = present(tile, new_u)
                    flow[target, slot, 1, here] = present(tile, new_v)
                    flow[target, slot, 2, here] = present(tile, new_h)

    @pl.loop(0, GROUPS)
    def _(group):
        for north in (True, False):
            when_receives(north, lambda: lat_copies(group, north).wait_recv())
        for var in range(3):
            for tile in range(4):
                rows = pl.ds(8 + 8 * tile, 8)
                total = jnp.zeros((8, 128), jnp.float32)
                for local in range(GROUP):
                    member = group * GROUP + local
                    flow[0, local, var, rows] = shifted_main(group, member, local, var, tile)
                    total = strip_part(total, group, member, local, var, local, tile)
                flow[0, GROUP, var, rows] = present(tile, total)

        @pl.loop(0, STEPS // 2 - 1)
        def _(pair):
            advance(0, 1, range(4))
            advance(1, 0, range(4))

        advance(0, 1, range(4))
        advance(1, 0, (1, 2))
        for local in range(GROUP):
            for var in range(3):
                for tile in range(2):
                    rows = pl.ds(16 + 8 * tile, 8)
                    main = roll(flow[0, local, var, rows], -WIDTH)
                    side = roll(flow[0, GROUP, var, rows], 128 - EDGE - local * STRIP)
                    at = pl.multiple_of((group * GROUP + local) * 48 + var * 16 + tile * 8, 8)
                    evolved[pl.ds(at, 8), :] = jnp.where(lane8 < 128 - 2 * WIDTH, main, side)

    flat = jnp.concatenate([evolved[pl.ds(j, 16, stride=48), :] for j in range(48)], axis=1)
    gram = lax.dot_general(
        flat,
        flat,
        (((1,), (1,)), ((), ())),
        precision=lax.Precision.HIGHEST,
        preferred_element_type=jnp.float32,
    )
    table[0:16, :] = jnp.zeros((16, 128), jnp.float32)
    table[0:16, 0:16] = gram
    row_id, lane = rows_of(16), lane16
    wide = table[0:16, :]
    wide = wide + roll(jnp.where((lane >= 8) & (lane < 12), wide, 0.0), 4)
    for shift in (16, 32, 64):
        wide = wide + roll(wide, shift)
    upper = (row_id < 8) & (lane // 16 == row_id) & (lane % 16 < 12)
    lower = (row_id >= 8) & (row_id < 12) & (lane // 16 == row_id - 8) & (lane % 16 >= 12)
    pick = upper | lower
    packed = jnp.sum(jnp.where(pick, wide, 0.0), axis=0, keepdims=True)

    def exchange(value, slot, buffer, me, count, peer_of, me_of, send, recv):
        row_out[slot] = value
        buffer[me] = value

        def copy(step, place):
            return pltpu.make_async_remote_copy(
                src_ref=row_out.at[slot],
                dst_ref=buffer.at[place],
                send_sem=send.at[step],
                recv_sem=recv.at[place],
                device_id=peer_of(step),
            )

        @pl.loop(1, count)
        def _(step):
            copy(step, me).start()

        @pl.loop(1, count)
        def _(step):
            copy(step, (me + step) % count).wait_recv()

        @pl.loop(1, count)
        def _(step):
            copy(step, me).wait_send()

        total = buffer[0]
        for index in range(1, count):
            total = total + buffer[index]
        return total

    packed = exchange(packed, 0, plane_in, me_plane, n_plane, plane_peer, None, plane_send, plane_recv)
    packed = exchange(packed, 1, column_in, level, n_level, column_peer, None, column_send, column_recv)

    cells = float(3 * 16 * n_lat * 128 * n_lon)
    work = jnp.broadcast_to(packed / cells, (16, 128))
    for bit in range(3):
        work = jnp.where((row_id // (1 << bit)) % 2 == 1, roll(work, -(16 << bit)), work)
    work = jnp.where(row_id >= 8, roll(work, -4), work)
    turned = jnp.transpose(work)[0:16, :]
    table[0:16, 0:16] = turned
    turned = table[0:16, :]
    work = jnp.where((row_id >= 8) & (lane < 8), turned, work)
    work = jnp.where((lane < 12) & (row_id < 12), work, 0.0)
    work = jnp.where((lane == row_id + 16) & (row_id < 12), 1.0, work)
    for k in range(MEMBERS - 1):
        pivot_row = work[k : k + 1, :]
        scaled = pivot_row / work[k : k + 1, k : k + 1]
        work = work - jnp.where(row_id > k, work[:, k : k + 1], 0.0) * scaled
    diagonal = jnp.sum(jnp.where(lane == row_id, work, 0.0), axis=1, keepdims=True)
    diagonal = jnp.where(row_id[:, 0:1] < MEMBERS, diagonal, 1.0)
    work = work / jnp.sqrt(diagonal)
    factor_ref[...] = jnp.where(lane >= row_id, work, 0.0)[0:MEMBERS, 0:MEMBERS]
    for k in range(MEMBERS):
        table[16 * k : 16 * k + 16, :] = jnp.broadcast_to(work[:, 16 + k : 17 + k], (16, 128))

    for var in range(3):
        for tile in range(2):
            inputs = [
                evolved[48 * m + 16 * var + 8 * tile : 48 * m + 16 * var + 8 * tile + 8, :]
                for m in range(MEMBERS)
            ]
            for m in range(MEMBERS):
                total = None
                for k in range(m + 1):
                    term = jnp.broadcast_to(table[16 * k + m : 16 * k + m + 1, :], (8, 128)) * inputs[k]
                    total = term if total is None else total + term
                fields_ref[m, var, 8 * tile : 8 * tile + 8, :] = total

    for piece in ("wind", "height", 0, 1, 2):
        for north in (True, False):
            when_sends(north, lambda: lat_copies(piece, north).wait_send())
    for to_east in (True, False):
        strip_copy(to_east, 0).wait_send()
        pl.when(has_north)(lambda: strip_copy(to_east, 1).wait_send())
        pl.when(has_south)(lambda: strip_copy(to_east, -1).wait_send())


def solution(mesh):
    n_lon, n_lat = mesh.shape["lon"], mesh.shape["lat"]
    n_plane, n_level = 2 * n_lat, n_lon // 2
    dma = pltpu.SemaphoreType.DMA

    def step(perturbations, base_wind, base_height):
        return pl.pallas_call(
            functools.partial(kernel, n_lon, n_lat),
            out_shape=(
                jax.ShapeDtypeStruct((MEMBERS, 3, 16, 128), jnp.float32),
                jax.ShapeDtypeStruct((MEMBERS, MEMBERS), jnp.float32),
            ),
            in_specs=[pl.BlockSpec(memory_space=pl.ANY)] * 3,
            out_specs=(pl.BlockSpec(memory_space=pltpu.VMEM), pl.BlockSpec(memory_space=pltpu.VMEM)),
            scratch_shapes=[
                pltpu.VMEM((MEMBERS + 1, 3, 32, 128), jnp.float32),
                pltpu.VMEM((GROUPS, 16, 128), jnp.float32),
                pltpu.VMEM((GROUPS, 16, 128), jnp.float32),
                pltpu.VMEM((GROUPS, 32, 128), jnp.float32),
                pltpu.VMEM((GROUPS, 32, 128), jnp.float32),
                pltpu.VMEM((2, GROUP + 1, 3, 48, 128), jnp.float32),
                pltpu.VMEM((2, 3, 48, 128), jnp.float32),
                pltpu.VMEM((COEFS, 2, 32, 128), jnp.float32),
                pltpu.VMEM((16 * 48, 128), jnp.float32),
                pltpu.VMEM((16 * MEMBERS, 128), jnp.float32),
                pltpu.VMEM((2, 1, 128), jnp.float32),
                pltpu.VMEM((n_plane, 1, 128), jnp.float32),
                pltpu.VMEM((n_level, 1, 128), jnp.float32),
                dma((3,)),
                dma((2, GROUPS + 2)),
                dma((2, GROUPS + 2)),
                dma((6,)),
                dma((6,)),
                dma((n_plane,)),
                dma((n_plane,)),
                dma((n_level,)),
                dma((n_level,)),
            ],
            compiler_params=pltpu.CompilerParams(collective_id=0, has_side_effects=True),
        )(perturbations, base_wind, base_height)

    return jax.shard_map(
        step,
        mesh=mesh,
        in_specs=(P(None, None, "lat", "lon"), P(None, "lat", "lon"), P("lat", "lon")),
        out_specs=(P(None, None, "lat", "lon"), P()),
        check_vma=False,
    )
```

```python
import functools
import math

import jax
import jax.numpy as jnp
from jax import lax
from jax.experimental import pallas as pl
from jax.experimental.pallas import tpu as pltpu
from jax.sharding import PartitionSpec as P

MEMBERS = 12
STEPS = 8
GROUP = 4
GROUPS = MEMBERS // GROUP
WIDTH = 8
EDGE = 24
STRIP = 32

advect_rate = 0.1
turn_rate = 0.5
gravity_rate = 0.2
diffuse_rate = 0.12

HALF = 0.5 * advect_rate
KEEP = 1.0 - 4.0 * diffuse_rate
PULL = 0.5 * gravity_rate
COEFS = 15


def roll(value, shift):
    shift = shift % 128
    return value if shift == 0 else pltpu.roll(value, shift, 1)


def lanes_of(rows):
    return lax.broadcasted_iota(jnp.int32, (rows, 128), 1)


def rows_of(rows):
    return lax.broadcasted_iota(jnp.int32, (rows, 128), 0)


def slot_of(local, var):
    return STRIP * local + WIDTH * var if local < GROUP else STRIP * var + EDGE


def kernel(
    n_lon,
    n_lat,
    x_hbm,
    wind_hbm,
    height_hbm,
    fields_ref,
    factor_ref,
    ext,
    send_low,
    send_high,
    from_west,
    from_east,
    flow,
    base,
    coef,
    evolved,
    table,
    row_out,
    plane_in,
    column_in,
    turns,
    load_sem,
    lat_send,
    lat_recv,
    strip_send,
    strip_recv,
    plane_send,
    plane_recv,
    column_send,
    column_recv,
    plane_known,
    level_known,
):
    lon = lax.axis_index("lon")
    lat = lax.axis_index("lat")
    level = lon // 2
    core = lon % 2
    n_level = n_lon // 2
    n_plane = 2 * n_lat
    me_plane = lat * 2 + core
    east = (lon + 1) % n_lon
    west = (lon + n_lon - 1) % n_lon
    has_south = lat > 0
    has_north = lat < n_lat - 1

    def device(lon_index, lat_index):
        return {"lon": lon_index, "lat": lat_index}

    loads = [
        pltpu.make_async_copy(x_hbm, ext.at[0:MEMBERS, :, 8:24], load_sem.at[0]),
        pltpu.make_async_copy(wind_hbm, ext.at[MEMBERS, 0:2, 8:24], load_sem.at[1]),
        pltpu.make_async_copy(height_hbm, ext.at[MEMBERS, 2, 8:24], load_sem.at[2]),
    ]
    for load in loads:
        load.start()

    def plane_peer(step):
        index = me_plane ^ step
        return device(level * 2 + (index & 1), index >> 1)

    def column_peer(step):
        return device((level ^ step) * 2 + core, lat)

    def level_peer(step):
        return device(((level + step) & (n_level - 1)) * 2 + core, lat)

    barrier = pltpu.get_barrier_semaphore()
    across = jnp.where(core == 1, east, west)
    mate = lon ^ 1
    near = [plane_peer(step) for step in (1, 2, 3, 4, 5, 6, 7, 8, 16, 24)]
    near += [level_peer(1), level_peer(-1), device(across, lat)]
    for peer in near:
        pl.semaphore_signal(barrier, inc=1, device_id=peer)
    for there, row in ((has_south, lat - 1), (has_north, lat + 1)):

        @pl.when(there)
        def _():
            for column in (lon, across, mate):
                pl.semaphore_signal(barrier, inc=1, device_id=device(column, row))

    for tile in range(4):
        place = (lat * 16 - 8 + 8 * tile + rows_of(8)).astype(jnp.float32)
        turns[8 * tile : 8 * tile + 8, :] = turn_rate * jnp.sin(math.pi * ((place + 0.5) / (16 * n_lat) - 0.5))
    evolved[MEMBERS * 48 :, :] = jnp.zeros((4 * 48, 128), jnp.float32)
    for parity in range(2):
        for slot in range(GROUP + 1):
            for var in range(3):
                flow[parity, slot, var, 0:8] = jnp.zeros((8, 128), jnp.float32)
                flow[parity, slot, var, 40:48] = jnp.zeros((8, 128), jnp.float32)
    for kind in range(2):
        for var in range(3):
            base[kind, var, 0:8] = jnp.zeros((8, 128), jnp.float32)
            base[kind, var, 40:48] = jnp.zeros((8, 128), jnp.float32)

    def lat_copies(piece, north):
        rows = pl.ds(8, 8) if north else pl.ds(0, 8)
        place = pl.ds(0, 8) if north else pl.ds(24, 8)
        way = 0 if north else 1
        target = device(lon, lat + 1 if north else lat - 1)
        if piece == "wind":
            source, goal, sem = wind_hbm.at[:, rows], ext.at[MEMBERS, 0:2, place], GROUPS
        elif piece == "height":
            source, goal, sem = height_hbm.at[rows], ext.at[MEMBERS, 2, place], GROUPS + 1
        else:
            members = pl.ds(piece * GROUP, GROUP)
            source, goal, sem = x_hbm.at[members, :, rows], ext.at[members, :, place], piece
        return pltpu.make_async_remote_copy(
            src_ref=source,
            dst_ref=goal,
            send_sem=lat_send.at[way, sem],
            recv_sem=lat_recv.at[way, sem],
            device_id=target,
        )

    def strip_copy(to_east, shift):
        packed = send_high if to_east else send_low
        goal = from_west if to_east else from_east
        rows = {0: pl.ds(0, 16), 1: pl.ds(8, 8), -1: pl.ds(0, 8)}[shift]
        place = {0: pl.ds(8, 16), 1: pl.ds(0, 8), -1: pl.ds(24, 8)}[shift]
        sem = (0 if to_east else 3) + shift + 1
        return pltpu.make_async_remote_copy(
            src_ref=packed.at[:, rows],
            dst_ref=goal.at[:, place],
            send_sem=strip_send.at[sem],
            recv_sem=strip_recv.at[sem],
            device_id=device(east if to_east else west, lat + shift),
        )

    def when_sends(north, body):
        pl.when(has_north if north else has_south)(body)

    def when_receives(north, body):
        pl.when(has_south if north else has_north)(body)

    lane8 = lanes_of(8)

    for load in loads:
        load.wait()

    lane16 = lanes_of(16)

    @pl.loop(0, GROUPS)
    def _(group):
        low = jnp.zeros((16, 128), jnp.float32)
        high = jnp.zeros((16, 128), jnp.float32)
        for local in range(GROUP + 1):
            for var in range(3):
                value = ext[group * GROUP + local if local < GROUP else MEMBERS, var, pl.ds(8, 16)]
                slot = slot_of(local, var)
                inside = (lane16 >= slot) & (lane16 < slot + WIDTH)
                low = jnp.where(inside, roll(value, slot), low)
                high = jnp.where(inside, roll(value, slot - 120), high)
        send_low[group] = low
        send_high[group] = high

    pl.semaphore_wait(
        barrier,
        len(near) + 3 * (has_south.astype(jnp.int32) + has_north.astype(jnp.int32)),
    )
    for step in (8, 16, 24):
        pl.semaphore_signal(plane_known, inc=1, device_id=plane_peer(step))
    for step in (1, -1):
        pl.semaphore_signal(level_known.at[0], inc=1, device_id=level_peer(step))

    for piece in ("wind", "height"):
        for north in (True, False):
            when_sends(north, lambda: lat_copies(piece, north).start())
    for to_east in (True, False):
        strip_copy(to_east, 0).start()
        pl.when(has_north)(lambda: strip_copy(to_east, 1).start())
        pl.when(has_south)(lambda: strip_copy(to_east, -1).start())
    for piece in range(GROUPS):
        for north in (True, False):
            when_sends(north, lambda: lat_copies(piece, north).start())

    pl.semaphore_wait(level_known.at[0], 2)
    for step in (2, -2):
        pl.semaphore_signal(level_known.at[1], inc=1, device_id=level_peer(step))

    for piece in ("wind", "height"):
        for north in (True, False):
            when_receives(north, lambda: lat_copies(piece, north).wait_recv())
    for to_east in (True, False):
        strip_copy(to_east, 0).wait_recv()
        pl.when(has_south)(lambda: strip_copy(to_east, 1).wait_recv())
        pl.when(has_north)(lambda: strip_copy(to_east, -1).wait_recv())

    def present(tile, value):
        if tile == 0:
            return jnp.where(has_south, value, 0.0)
        if tile == 3:
            return jnp.where(has_north, value, 0.0)
        return value

    def rows_at(tile):
        return pl.ds(8 * tile, 8)

    def main_part(group, member, local, var, tile):
        rim = roll(from_west[group, rows_at(tile)], 128 - WIDTH - slot_of(local, var))
        return present(tile, jnp.where(lane8 < 128 - WIDTH, ext[member, var, rows_at(tile)], rim))

    def strip_own(total, member, var, place, tile):
        own = roll(ext[member, var, rows_at(tile)], STRIP * place + WIDTH - (128 - EDGE))
        return own if total is None else jnp.where((lane8 >= STRIP * place + WIDTH), own, total)

    for var in range(3):
        for tile in range(4):
            rows = pl.ds(8 + 8 * tile, 8)
            base[0, var, rows] = main_part(0, MEMBERS, GROUP, var, tile)
            total = None
            for place in range(4):
                total = strip_own(total, MEMBERS, var, place, tile)
            for place in range(4):
                rim = roll(from_east[0, rows_at(tile)], STRIP * (place + 1) - slot_of(GROUP, var))
                first = STRIP * ((place + 1) % 4)
                total = jnp.where((lane8 >= first) & (lane8 < first + WIDTH), rim, total)
            base[1, var, rows] = present(tile, total)
    for tile in range(4):
        turning = turns[8 * tile : 8 * tile + 8, :]
        for kind in range(2):
            here, up, down = pl.ds(8 + 8 * tile, 8), pl.ds(9 + 8 * tile, 8), pl.ds(7 + 8 * tile, 8)
            mean_x = base[kind, 0, here]
            mean_y = base[kind, 1, here]
            depth = base[kind, 2, here]
            x_up, x_down = base[kind, 0, up], base[kind, 0, down]
            y_up, y_down = base[kind, 1, up], base[kind, 1, down]
            x_east, x_west = roll(mean_x, -1), roll(mean_x, 1)
            values = [
                diffuse_rate - HALF * x_west,
                diffuse_rate + HALF * x_east,
                diffuse_rate - HALF * mean_x,
                diffuse_rate + HALF * mean_x,
                present(tile, diffuse_rate - HALF * mean_y),
                present(tile, diffuse_rate + HALF * mean_y),
                KEEP - HALF * (x_east - x_west),
                turning - HALF * (x_up - x_down),
                KEEP - HALF * (y_up - y_down),
                -turning - HALF * (roll(mean_y, -1) - roll(mean_y, 1)),
                (PULL * HALF) * depth,
                present(tile, diffuse_rate - HALF * y_up),
                present(tile, diffuse_rate + HALF * y_down),
                present(tile, (PULL * HALF) * base[kind, 2, up]),
                present(tile, (PULL * HALF) * base[kind, 2, down]),
            ]
            for index, value in enumerate(values):
                coef[index, kind, pl.ds(8 * tile, 8)] = value

    def advance(source, target, tiles):
        for tile in tiles:
            here, up, down = pl.ds(8 + 8 * tile, 8), pl.ds(9 + 8 * tile, 8), pl.ds(7 + 8 * tile, 8)
            for kind, slots in ((0, range(GROUP)), (1, (GROUP,))):
                (e, w, e_h, w_h, n, s, keep_x, turn_x, keep_y, turn_y, deep, n_h, s_h, n_deep, s_deep) = [
                    coef[index, kind, rows_at(tile)] for index in range(COEFS)
                ]
                for slot in slots:
                    u, u_n, u_s = (flow[source, slot, 0, r] for r in (here, up, down))
                    v, v_n, v_s = (flow[source, slot, 1, r] for r in (here, up, down))
                    h, h_n, h_s = (flow[source, slot, 2, r] for r in (here, up, down))
                    carried = deep * u
                    flow[target, slot, 0, here] = (
                        (keep_x * u + turn_x * v)
                        + (n * u_n + s * u_s)
                        + (roll(e * u - h, -1) + roll(w * u + h, 1))
                    )
                    flow[target, slot, 1, here] = (
                        (keep_y * v + turn_y * u)
                        + (n * v_n + s * v_s)
                        + (roll(e * v, -1) + roll(w * v, 1))
                        - present(tile, h_n - h_s)
                    )
                    flow[target, slot, 2, here] = (
                        KEEP * h
                        + (roll(e_h * h - carried, -1) + roll(w_h * h + carried, 1))
                        + (n_h * h_n + s_h * h_s)
                        - (n_deep * v_n - s_deep * v_s)
                    )

    pl.semaphore_wait(level_known.at[1], 2)
    for step in (4, -4):
        pl.semaphore_signal(level_known.at[2], inc=1, device_id=level_peer(step))

    @pl.loop(0, GROUPS)
    def _(group):
        for north in (True, False):
            when_receives(north, lambda: lat_copies(group, north).wait_recv())
        for var in range(3):
            for tile in range(4):
                rows = pl.ds(8 + 8 * tile, 8)
                scale = PULL if var == 2 else 1.0
                total = None
                for local in range(GROUP):
                    member = group * GROUP + local
                    flow[0, local, var, rows] = main_part(group, member, local, var, tile) * scale
                    total = strip_own(total, member, var, local, tile)
                rim = roll(from_east[group, rows_at(tile)], STRIP - WIDTH * var)
                total = jnp.where(lane8 % STRIP < WIDTH, rim, total)
                flow[0, GROUP, var, rows] = present(tile, total) * scale

        @pl.loop(0, STEPS // 2 - 1)
        def _(pair):
            advance(0, 1, range(4))
            advance(1, 0, range(4))

        advance(0, 1, range(4))
        advance(1, 0, (1, 2))
        for local in range(GROUP):
            for var in range(3):
                for tile in range(2):
                    rows = pl.ds(16 + 8 * tile, 8)
                    main = flow[0, local, var, rows]
                    side = roll(flow[0, GROUP, var, rows], 128 - STRIP * (local + 1))
                    at = pl.multiple_of((group * GROUP + local) * 48 + var * 16 + tile * 8, 8)
                    evolved[pl.ds(at, 8), :] = (
                        jnp.where(lane8 < 128 - 2 * WIDTH, main, side) * (1.0 / PULL if var == 2 else 1.0)
                    )

    flat = jnp.concatenate([evolved[pl.ds(j, 16, stride=48), :] for j in range(48)], axis=1)
    gram = lax.dot_general(
        flat,
        flat,
        (((1,), (1,)), ((), ())),
        precision=lax.Precision.HIGHEST,
        preferred_element_type=jnp.float32,
    )
    table[0:16, :] = jnp.zeros((16, 128), jnp.float32)
    table[0:16, 0:16] = gram
    row_id, lane = rows_of(16), lane16
    wide = table[0:16, :]
    wide = wide + roll(jnp.where((lane >= 8) & (lane < 12), wide, 0.0), 4)
    for shift in (16, 32, 64):
        wide = wide + roll(wide, shift)
    upper = (row_id < 8) & (lane // 16 == row_id) & (lane % 16 < 12)
    lower = (row_id >= 8) & (row_id < 12) & (lane // 16 == row_id - 8) & (lane % 16 >= 12)
    pick = upper | lower
    packed = jnp.sum(jnp.where(pick, wide, 0.0), axis=0, keepdims=True)

    def exchange_copy(slot, step, place):
        buffer, peer_of, send, recv = (
            (plane_in, plane_peer, plane_send, plane_recv),
            (column_in, column_peer, column_send, column_recv),
        )[slot]
        return pltpu.make_async_remote_copy(
            src_ref=row_out.at[slot],
            dst_ref=buffer.at[place],
            send_sem=send.at[step],
            recv_sem=recv.at[place],
            device_id=peer_of(step),
        )

    def exchange(value, slot, buffer, me, order):
        row_out[slot] = value
        buffer[me] = value
        for step in order:
            exchange_copy(slot, step, me).start()
        for step in reversed(order):
            exchange_copy(slot, step, me ^ step).wait_recv()
        parts = [buffer[index] for index in range(len(order) + 1)]
        while len(parts) > 1:
            parts = [a + b for a, b in zip(parts[0::2], parts[1::2])]
        return parts[0]

    def hops(step):
        pair = {0: 0, 1: 1, 2: 2, 3: 1}
        return pair[(step >> 1) & 3] + pair[(step >> 3) & 3]

    plane_order = sorted(range(1, n_plane), key=lambda step: -hops(step))
    column_order = sorted(range(1, n_level), key=lambda step: -min(step, n_level - step))

    pl.semaphore_wait(plane_known, 3)
    packed = exchange(packed, 0, plane_in, me_plane, plane_order)
    pl.semaphore_wait(level_known.at[2], 2)
    packed = exchange(packed, 1, column_in, level, column_order)

    cells = float(3 * 16 * n_lat * 128 * n_lon)
    work = jnp.broadcast_to(packed / cells, (16, 128))
    for bit in range(3):
        work = jnp.where((row_id // (1 << bit)) % 2 == 1, roll(work, -(16 << bit)), work)
    work = jnp.where(row_id >= 8, roll(work, -4), work)
    turned = jnp.transpose(work)[0:16, :]
    table[0:16, 0:16] = turned
    turned = table[0:16, :]
    work = jnp.where((row_id >= 8) & (lane < 8), turned, work)
    work = jnp.where((lane < 12) & (row_id < 12), work, 0.0)
    work = jnp.where((lane == row_id + 16) & (row_id < 12), 1.0, work)
    for k in range(MEMBERS - 1):
        pivot_row = work[k : k + 1, :]
        scaled = pivot_row / work[k : k + 1, k : k + 1]
        work = work - jnp.where(row_id > k, work[:, k : k + 1], 0.0) * scaled
    diagonal = jnp.sum(jnp.where(lane == row_id, work, 0.0), axis=1, keepdims=True)
    diagonal = jnp.where(row_id[:, 0:1] < MEMBERS, diagonal, 1.0)
    work = work / jnp.sqrt(diagonal)
    factor_ref[...] = jnp.where(lane >= row_id, work, 0.0)[0:MEMBERS, 0:MEMBERS]
    for k in range(MEMBERS):
        table[16 * k : 16 * k + 16, :] = jnp.broadcast_to(work[:, 16 + k : 17 + k], (16, 128))

    for var in range(3):
        for tile in range(2):
            inputs = [
                evolved[48 * m + 16 * var + 8 * tile : 48 * m + 16 * var + 8 * tile + 8, :]
                for m in range(MEMBERS)
            ]
            for m in range(MEMBERS):
                total = None
                for k in range(m + 1):
                    term = jnp.broadcast_to(table[16 * k + m : 16 * k + m + 1, :], (8, 128)) * inputs[k]
                    total = term if total is None else total + term
                fields_ref[m, var, 8 * tile : 8 * tile + 8, :] = total

    for piece in ("wind", "height", 0, 1, 2):
        for north in (True, False):
            when_sends(north, lambda: lat_copies(piece, north).wait_send())
    for to_east in (True, False):
        strip_copy(to_east, 0).wait_send()
        pl.when(has_north)(lambda: strip_copy(to_east, 1).wait_send())
        pl.when(has_south)(lambda: strip_copy(to_east, -1).wait_send())
    for step in plane_order:
        exchange_copy(0, step, me_plane).wait_send()
    for step in column_order:
        exchange_copy(1, step, level).wait_send()


def solution(mesh):
    n_lon, n_lat = mesh.shape["lon"], mesh.shape["lat"]
    n_plane, n_level = 2 * n_lat, n_lon // 2
    dma = pltpu.SemaphoreType.DMA

    def step(perturbations, base_wind, base_height):
        return pl.pallas_call(
            functools.partial(kernel, n_lon, n_lat),
            out_shape=(
                jax.ShapeDtypeStruct((MEMBERS, 3, 16, 128), jnp.float32),
                jax.ShapeDtypeStruct((MEMBERS, MEMBERS), jnp.float32),
            ),
            in_specs=[pl.BlockSpec(memory_space=pl.ANY)] * 3,
            out_specs=(pl.BlockSpec(memory_space=pltpu.VMEM), pl.BlockSpec(memory_space=pltpu.VMEM)),
            scratch_shapes=[
                pltpu.VMEM((MEMBERS + 1, 3, 32, 128), jnp.float32),
                pltpu.VMEM((GROUPS, 16, 128), jnp.float32),
                pltpu.VMEM((GROUPS, 16, 128), jnp.float32),
                pltpu.VMEM((GROUPS, 32, 128), jnp.float32),
                pltpu.VMEM((GROUPS, 32, 128), jnp.float32),
                pltpu.VMEM((2, GROUP + 1, 3, 48, 128), jnp.float32),
                pltpu.VMEM((2, 3, 48, 128), jnp.float32),
                pltpu.VMEM((COEFS, 2, 32, 128), jnp.float32),
                pltpu.VMEM((16 * 48, 128), jnp.float32),
                pltpu.VMEM((16 * MEMBERS, 128), jnp.float32),
                pltpu.VMEM((2, 1, 128), jnp.float32),
                pltpu.VMEM((n_plane, 1, 128), jnp.float32),
                pltpu.VMEM((n_level, 1, 128), jnp.float32),
                pltpu.VMEM((32, 128), jnp.float32),
                dma((3,)),
                dma((2, GROUPS + 2)),
                dma((2, GROUPS + 2)),
                dma((6,)),
                dma((6,)),
                dma((n_plane,)),
                dma((n_plane,)),
                dma((n_level,)),
                dma((n_level,)),
                pltpu.SemaphoreType.REGULAR,
                pltpu.SemaphoreType.REGULAR((3,)),
            ],
            compiler_params=pltpu.CompilerParams(collective_id=0, has_side_effects=True),
        )(perturbations, base_wind, base_height)

    return jax.shard_map(
        step,
        mesh=mesh,
        in_specs=(P(None, None, "lat", "lon"), P(None, "lat", "lon"), P("lat", "lon")),
        out_specs=(P(None, None, "lat", "lon"), P()),
        check_vma=False,
    )
```

```python
import functools
import math

import jax
import jax.numpy as jnp
from jax import lax
from jax.experimental import pallas as pl
from jax.experimental.pallas import tpu as pltpu
from jax.sharding import PartitionSpec as P

MEMBERS = 12
STEPS = 8
GROUP = 4
GROUPS = MEMBERS // GROUP
WIDTH = 8
EDGE = 24
STRIP = 32

advect_rate = 0.1
turn_rate = 0.5
gravity_rate = 0.2
diffuse_rate = 0.12

HALF = 0.5 * advect_rate
KEEP = 1.0 - 4.0 * diffuse_rate
PULL = 0.5 * gravity_rate
COEFS = 16


def roll(value, shift):
    shift = shift % 128
    return value if shift == 0 else pltpu.roll(value, shift, 1)


def lanes_of(rows):
    return lax.broadcasted_iota(jnp.int32, (rows, 128), 1)


def rows_of(rows):
    return lax.broadcasted_iota(jnp.int32, (rows, 128), 0)


def slot_of(local, var):
    return STRIP * local + WIDTH * var if local < GROUP else STRIP * var + EDGE


def kernel(
    n_lon,
    n_lat,
    x_hbm,
    wind_hbm,
    height_hbm,
    evolved,
    row_ref,
    ext,
    send_low,
    send_high,
    from_west,
    from_east,
    flow,
    base,
    coef,
    table,
    row_out,
    plane_in,
    column_in,
    turns,
    load_sem,
    lat_send,
    lat_recv,
    strip_send,
    strip_recv,
    plane_send,
    plane_recv,
    column_send,
    column_recv,
    plane_known,
    level_known,
):
    lon = lax.axis_index("lon")
    lat = lax.axis_index("lat")
    level = lon // 2
    core = lon % 2
    n_level = n_lon // 2
    n_plane = 2 * n_lat
    me_plane = lat * 2 + core
    east = (lon + 1) % n_lon
    west = (lon + n_lon - 1) % n_lon
    has_south = lat > 0
    has_north = lat < n_lat - 1

    def device(lon_index, lat_index):
        return {"lon": lon_index, "lat": lat_index}

    loads = [
        pltpu.make_async_copy(x_hbm, ext.at[0:MEMBERS, :, 8:24], load_sem.at[0]),
        pltpu.make_async_copy(wind_hbm, ext.at[MEMBERS, 0:2, 8:24], load_sem.at[1]),
        pltpu.make_async_copy(height_hbm, ext.at[MEMBERS, 2, 8:24], load_sem.at[2]),
    ]
    for load in loads:
        load.start()

    def plane_peer(step):
        index = me_plane ^ step
        return device(level * 2 + (index & 1), index >> 1)

    def column_peer(step):
        return device((level ^ step) * 2 + core, lat)

    def level_peer(step):
        return device(((level + step) & (n_level - 1)) * 2 + core, lat)

    barrier = pltpu.get_barrier_semaphore()
    across = jnp.where(core == 1, east, west)
    mate = lon ^ 1
    near = [plane_peer(step) for step in (1, 2, 3, 4, 5, 6, 7, 8, 16, 24)]
    near += [level_peer(1), level_peer(-1), device(across, lat)]
    for peer in near:
        pl.semaphore_signal(barrier, inc=1, device_id=peer)
    for there, row in ((has_south, lat - 1), (has_north, lat + 1)):

        @pl.when(there)
        def _():
            for column in (lon, across, mate):
                pl.semaphore_signal(barrier, inc=1, device_id=device(column, row))

    for tile in range(4):
        place = (lat * 16 - 8 + 8 * tile + rows_of(8)).astype(jnp.float32)
        turns[8 * tile : 8 * tile + 8, :] = turn_rate * jnp.sin(math.pi * ((place + 0.5) / (16 * n_lat) - 0.5))
    evolved[MEMBERS * 48 :, :] = jnp.zeros((4 * 48, 128), jnp.float32)
    for parity in range(2):
        for slot in range(GROUP + 1):
            for var in range(3):
                flow[parity, slot, var, 0:8] = jnp.zeros((8, 128), jnp.float32)
                flow[parity, slot, var, 40:48] = jnp.zeros((8, 128), jnp.float32)
    for kind in range(2):
        for var in range(3):
            base[kind, var, 0:8] = jnp.zeros((8, 128), jnp.float32)
            base[kind, var, 40:48] = jnp.zeros((8, 128), jnp.float32)

    def lat_copies(piece, north):
        rows = pl.ds(8, 8) if north else pl.ds(0, 8)
        place = pl.ds(0, 8) if north else pl.ds(24, 8)
        way = 0 if north else 1
        target = device(lon, lat + 1 if north else lat - 1)
        if piece == "wind":
            source, goal, sem = wind_hbm.at[:, rows], ext.at[MEMBERS, 0:2, place], GROUPS
        elif piece == "height":
            source, goal, sem = height_hbm.at[rows], ext.at[MEMBERS, 2, place], GROUPS + 1
        else:
            members = pl.ds(piece * GROUP, GROUP)
            source, goal, sem = x_hbm.at[members, :, rows], ext.at[members, :, place], piece
        return pltpu.make_async_remote_copy(
            src_ref=source,
            dst_ref=goal,
            send_sem=lat_send.at[way, sem],
            recv_sem=lat_recv.at[way, sem],
            device_id=target,
        )

    def strip_copy(to_east, shift):
        packed = send_high if to_east else send_low
        goal = from_west if to_east else from_east
        rows = {0: pl.ds(0, 16), 1: pl.ds(8, 8), -1: pl.ds(0, 8)}[shift]
        place = {0: pl.ds(8, 16), 1: pl.ds(0, 8), -1: pl.ds(24, 8)}[shift]
        sem = (0 if to_east else 3) + shift + 1
        return pltpu.make_async_remote_copy(
            src_ref=packed.at[:, rows],
            dst_ref=goal.at[:, place],
            send_sem=strip_send.at[sem],
            recv_sem=strip_recv.at[sem],
            device_id=device(east if to_east else west, lat + shift),
        )

    def when_sends(north, body):
        pl.when(has_north if north else has_south)(body)

    def when_receives(north, body):
        pl.when(has_south if north else has_north)(body)

    lane8 = lanes_of(8)

    pl.semaphore_wait(
        barrier,
        len(near) + 3 * (has_south.astype(jnp.int32) + has_north.astype(jnp.int32)),
    )
    for step in (8, 16, 24):
        pl.semaphore_signal(plane_known, inc=1, device_id=plane_peer(step))
    for step in (1, -1):
        pl.semaphore_signal(level_known.at[0], inc=1, device_id=level_peer(step))

    for piece in ("wind", "height", 0):
        for north in (True, False):
            when_sends(north, lambda: lat_copies(piece, north).start())

    for load in loads:
        load.wait()

    lane16 = lanes_of(16)

    @pl.loop(0, GROUPS)
    def _(group):
        low = jnp.zeros((16, 128), jnp.float32)
        high = jnp.zeros((16, 128), jnp.float32)
        for local in range(GROUP + 1):
            for var in range(3):
                value = ext[group * GROUP + local if local < GROUP else MEMBERS, var, pl.ds(8, 16)]
                slot = slot_of(local, var)
                inside = (lane16 >= slot) & (lane16 < slot + WIDTH)
                low = jnp.where(inside, roll(value, slot), low)
                high = jnp.where(inside, roll(value, slot - 120), high)
        send_low[group] = low
        send_high[group] = high

    for to_east in (True, False):
        pl.when(has_north)(lambda: strip_copy(to_east, 1).start())
        pl.when(has_south)(lambda: strip_copy(to_east, -1).start())
        strip_copy(to_east, 0).start()
    for piece in range(1, GROUPS):
        for north in (True, False):
            when_sends(north, lambda: lat_copies(piece, north).start())

    pl.semaphore_wait(level_known.at[0], 2)
    for step in (2, -2):
        pl.semaphore_signal(level_known.at[1], inc=1, device_id=level_peer(step))

    for piece in ("wind", "height"):
        for north in (True, False):
            when_receives(north, lambda: lat_copies(piece, north).wait_recv())
    for to_east in (True, False):
        strip_copy(to_east, 0).wait_recv()
        pl.when(has_south)(lambda: strip_copy(to_east, 1).wait_recv())
        pl.when(has_north)(lambda: strip_copy(to_east, -1).wait_recv())

    def present(tile, value):
        if tile == 0:
            return jnp.where(has_south, value, 0.0)
        if tile == 3:
            return jnp.where(has_north, value, 0.0)
        return value

    def rows_at(tile):
        return pl.ds(8 * tile, 8)

    def main_part(group, member, local, var, tile):
        rim = roll(from_west[group, rows_at(tile)], 128 - WIDTH - slot_of(local, var))
        return present(tile, jnp.where(lane8 < 128 - WIDTH, ext[member, var, rows_at(tile)], rim))

    def strip_own(total, member, var, place, tile):
        own = roll(ext[member, var, rows_at(tile)], STRIP * place + WIDTH - (128 - EDGE))
        return own if total is None else jnp.where((lane8 >= STRIP * place + WIDTH), own, total)

    for var in range(3):
        for tile in range(4):
            rows = pl.ds(8 + 8 * tile, 8)
            base[0, var, rows] = main_part(0, MEMBERS, GROUP, var, tile)
            total = None
            for place in range(4):
                total = strip_own(total, MEMBERS, var, place, tile)
            for place in range(4):
                rim = roll(from_east[0, rows_at(tile)], STRIP * (place + 1) - slot_of(GROUP, var))
                first = STRIP * ((place + 1) % 4)
                total = jnp.where((lane8 >= first) & (lane8 < first + WIDTH), rim, total)
            base[1, var, rows] = present(tile, total)
    for tile in range(4):
        turning = turns[8 * tile : 8 * tile + 8, :]
        for kind in range(2):
            here, up, down = pl.ds(8 + 8 * tile, 8), pl.ds(9 + 8 * tile, 8), pl.ds(7 + 8 * tile, 8)
            mean_x = base[kind, 0, here]
            mean_y = base[kind, 1, here]
            depth = base[kind, 2, here]
            x_up, x_down = base[kind, 0, up], base[kind, 0, down]
            y_up, y_down = base[kind, 1, up], base[kind, 1, down]
            x_east, x_west = roll(mean_x, -1), roll(mean_x, 1)
            values = [
                diffuse_rate - HALF * x_west,
                diffuse_rate + HALF * x_east,
                diffuse_rate - HALF * mean_x,
                diffuse_rate + HALF * mean_x,
                present(tile, diffuse_rate - HALF * mean_y),
                present(tile, diffuse_rate + HALF * mean_y),
                KEEP - HALF * (x_east - x_west),
                turning - HALF * (x_up - x_down),
                KEEP - HALF * (y_up - y_down),
                -turning - HALF * (roll(mean_y, -1) - roll(mean_y, 1)),
                (PULL * HALF) * depth,
                present(tile, diffuse_rate - HALF * y_up),
                present(tile, diffuse_rate + HALF * y_down),
                present(tile, (PULL * HALF) * base[kind, 2, up]),
                present(tile, (PULL * HALF) * base[kind, 2, down]),
                present(tile, jnp.ones((8, 128), jnp.float32)),
            ]
            for index, value in enumerate(values):
                coef[index, kind, pl.ds(8 * tile, 8)] = value

    def advance(source, target, starts):
        for start in starts:
            here, up, down = pl.ds(8 + start, 8), pl.ds(9 + start, 8), pl.ds(7 + start, 8)
            inner = 8 <= start <= 16
            for kind, slots in ((0, range(GROUP)), (1, (GROUP,))):
                (e, w, e_h, w_h, n, s, keep_x, turn_x, keep_y, turn_y, deep, n_h, s_h, n_deep, s_deep) = [
                    coef[index, kind, pl.ds(start, 8)] for index in range(COEFS - 1)
                ]
                slope = None if inner else coef[COEFS - 1, kind, pl.ds(start, 8)]
                for slot in slots:
                    u, u_n, u_s = (flow[source, slot, 0, r] for r in (here, up, down))
                    v, v_n, v_s = (flow[source, slot, 1, r] for r in (here, up, down))
                    h, h_n, h_s = (flow[source, slot, 2, r] for r in (here, up, down))
                    carried = deep * u
                    flow[target, slot, 0, here] = (
                        (keep_x * u + turn_x * v)
                        + (n * u_n + s * u_s)
                        + (roll(e * u - h, -1) + roll(w * u + h, 1))
                    )
                    flow[target, slot, 1, here] = (
                        (keep_y * v + turn_y * u)
                        + (n * v_n + s * v_s)
                        + (roll(e * v, -1) + roll(w * v, 1))
                        - (h_n - h_s if inner else slope * (h_n - h_s))
                    )
                    flow[target, slot, 2, here] = (
                        KEEP * h
                        + (roll(e_h * h - carried, -1) + roll(w_h * h + carried, 1))
                        + (n_h * h_n + s_h * h_s)
                        - (n_deep * v_n - s_deep * v_s)
                    )

    pl.semaphore_wait(level_known.at[1], 2)
    for step in (4, -4):
        pl.semaphore_signal(level_known.at[2], inc=1, device_id=level_peer(step))

    @pl.loop(0, GROUPS)
    def _(group):
        for north in (True, False):
            when_receives(north, lambda: lat_copies(group, north).wait_recv())
        for var in range(3):
            for tile in range(4):
                rows = pl.ds(8 + 8 * tile, 8)
                scale = PULL if var == 2 else 1.0
                total = None
                for local in range(GROUP):
                    member = group * GROUP + local
                    flow[0, local, var, rows] = main_part(group, member, local, var, tile) * scale
                    total = strip_own(total, member, var, local, tile)
                rim = roll(from_east[group, rows_at(tile)], STRIP - WIDTH * var)
                total = jnp.where(lane8 % STRIP < WIDTH, rim, total)
                flow[0, GROUP, var, rows] = present(tile, total) * scale

        for index in range(STEPS):
            starts = (0, 8, 16, 24) if index < 3 else (4, 12, 20) if index < 7 else (8, 16)
            advance(index % 2, 1 - index % 2, starts)
        for local in range(GROUP):
            for var in range(3):
                for tile in range(2):
                    rows = pl.ds(16 + 8 * tile, 8)
                    main = flow[0, local, var, rows]
                    side = roll(flow[0, GROUP, var, rows], 128 - STRIP * (local + 1))
                    at = pl.multiple_of((group * GROUP + local) * 48 + var * 16 + tile * 8, 8)
                    evolved[pl.ds(at, 8), :] = (
                        jnp.where(lane8 < 128 - 2 * WIDTH, main, side) * (1.0 / PULL if var == 2 else 1.0)
                    )

    flat = jnp.concatenate([evolved[pl.ds(j, 16, stride=48), :] for j in range(48)], axis=1)
    gram = lax.dot_general(
        flat,
        flat,
        (((1,), (1,)), ((), ())),
        precision=lax.Precision.HIGHEST,
        preferred_element_type=jnp.float32,
    )
    table[0:16, :] = jnp.zeros((16, 128), jnp.float32)
    table[0:16, 0:16] = gram
    row_id, lane = rows_of(16), lane16
    wide = table[0:16, :]
    wide = wide + roll(jnp.where((lane >= 8) & (lane < 12), wide, 0.0), 4)
    for shift in (16, 32, 64):
        wide = wide + roll(wide, shift)
    upper = (row_id < 8) & (lane // 16 == row_id) & (lane % 16 < 12)
    lower = (row_id >= 8) & (row_id < 12) & (lane // 16 == row_id - 8) & (lane % 16 >= 12)
    pick = upper | lower
    packed = jnp.sum(jnp.where(pick, wide, 0.0), axis=0, keepdims=True)

    def exchange_copy(slot, step, place):
        buffer, peer_of, send, recv = (
            (plane_in, plane_peer, plane_send, plane_recv),
            (column_in, column_peer, column_send, column_recv),
        )[slot]
        return pltpu.make_async_remote_copy(
            src_ref=row_out.at[slot],
            dst_ref=buffer.at[place],
            send_sem=send.at[step],
            recv_sem=recv.at[place],
            device_id=peer_of(step),
        )

    def exchange(value, slot, buffer, me, order, beside):
        row_out[slot] = value
        buffer[me] = value
        for step in order:
            exchange_copy(slot, step, me).start()
        beside()
        for step in reversed(order):
            exchange_copy(slot, step, me ^ step).wait_recv()
        parts = [buffer[index] for index in range(len(order) + 1)]
        while len(parts) > 1:
            parts = [a + b for a, b in zip(parts[0::2], parts[1::2])]
        return parts[0]

    def halo_sent():
        for piece in ("wind", "height", 0, 1, 2):
            for north in (True, False):
                when_sends(north, lambda: lat_copies(piece, north).wait_send())
        for to_east in (True, False):
            strip_copy(to_east, 0).wait_send()
            pl.when(has_north)(lambda: strip_copy(to_east, 1).wait_send())
            pl.when(has_south)(lambda: strip_copy(to_east, -1).wait_send())

    def plane_sent():
        for step in plane_order:
            exchange_copy(0, step, me_plane).wait_send()

    def hops(step):
        pair = {0: 0, 1: 1, 2: 2, 3: 1}
        return pair[(step >> 1) & 3] + pair[(step >> 3) & 3]

    plane_order = sorted(range(1, n_plane), key=lambda step: -hops(step))
    column_order = sorted(range(1, n_level), key=lambda step: -min(step, n_level - step))

    pl.semaphore_wait(plane_known, 3)
    packed = exchange(packed, 0, plane_in, me_plane, plane_order, halo_sent)
    pl.semaphore_wait(level_known.at[2], 2)
    packed = exchange(packed, 1, column_in, level, column_order, plane_sent)

    row_ref[...] = packed
    for step in column_order:
        exchange_copy(1, step, level).wait_send()


def finish(cells, evolved, row_ref, fields_hbm, factor_ref, table, out, sems):
    row_id, lane = rows_of(16), lanes_of(16)
    packed = row_ref[...]

    work = jnp.broadcast_to(packed / cells, (16, 128))
    for bit in range(3):
        work = jnp.where((row_id // (1 << bit)) % 2 == 1, roll(work, -(16 << bit)), work)
    work = jnp.where(row_id >= 8, roll(work, -4), work)
    turned = jnp.transpose(work)[0:16, :]
    table[0:16, 0:16] = turned
    turned = table[0:16, :]
    work = jnp.where((row_id >= 8) & (lane < 8), turned, work)
    work = jnp.where((lane < 12) & (row_id < 12), work, 0.0)
    work = jnp.where((lane == row_id + 16) & (row_id < 12), 1.0, work)
    for k in range(MEMBERS - 1):
        pivot_row = work[k : k + 1, :]
        scaled = pivot_row / work[k : k + 1, k : k + 1]
        work = work - jnp.where(row_id > k, work[:, k : k + 1], 0.0) * scaled
    diagonal = jnp.sum(jnp.where(lane == row_id, work, 0.0), axis=1, keepdims=True)
    diagonal = jnp.where(row_id[:, 0:1] < MEMBERS, diagonal, 1.0)
    work = work / jnp.sqrt(diagonal)
    factor_ref[...] = jnp.where(lane >= row_id, work, 0.0)[0:MEMBERS, 0:MEMBERS]
    for k in range(MEMBERS):
        table[16 * k : 16 * k + 16, :] = jnp.broadcast_to(work[:, 16 + k : 17 + k], (16, 128))

    def copy_out(member):
        return pltpu.make_async_copy(out.at[member], fields_hbm.at[member], sems.at[member])

    for m in range(MEMBERS):
        scale = [jnp.broadcast_to(table[16 * k + m : 16 * k + m + 1, :], (8, 128)) for k in range(m + 1)]
        for place in range(6):
            total = None
            for k in range(m + 1):
                term = scale[k] * evolved[48 * k + 8 * place : 48 * k + 8 * place + 8, :]
                total = term if total is None else total + term
            out[m, place // 2, 8 * (place % 2) : 8 * (place % 2) + 8, :] = total
        copy_out(m).start()
    for m in range(MEMBERS):
        copy_out(m).wait()


def solution(mesh):
    n_lon, n_lat = mesh.shape["lon"], mesh.shape["lat"]
    n_plane, n_level = 2 * n_lat, n_lon // 2
    dma = pltpu.SemaphoreType.DMA

    def step(perturbations, base_wind, base_height):
        evolved, row = pl.pallas_call(
            functools.partial(kernel, n_lon, n_lat),
            out_shape=(
                pltpu.VMEM((16 * 48, 128), jnp.float32),
                pltpu.VMEM((1, 128), jnp.float32),
            ),
            in_specs=[pl.BlockSpec(memory_space=pl.ANY)] * 3,
            out_specs=(pl.BlockSpec(memory_space=pltpu.VMEM), pl.BlockSpec(memory_space=pltpu.VMEM)),
            scratch_shapes=[
                pltpu.VMEM((MEMBERS + 1, 3, 32, 128), jnp.float32),
                pltpu.VMEM((GROUPS, 16, 128), jnp.float32),
                pltpu.VMEM((GROUPS, 16, 128), jnp.float32),
                pltpu.VMEM((GROUPS, 32, 128), jnp.float32),
                pltpu.VMEM((GROUPS, 32, 128), jnp.float32),
                pltpu.VMEM((2, GROUP + 1, 3, 48, 128), jnp.float32),
                pltpu.VMEM((2, 3, 48, 128), jnp.float32),
                pltpu.VMEM((COEFS, 2, 32, 128), jnp.float32),
                pltpu.VMEM((16, 128), jnp.float32),
                pltpu.VMEM((2, 1, 128), jnp.float32),
                pltpu.VMEM((n_plane, 1, 128), jnp.float32),
                pltpu.VMEM((n_level, 1, 128), jnp.float32),
                pltpu.VMEM((32, 128), jnp.float32),
                dma((3,)),
                dma((2, GROUPS + 2)),
                dma((2, GROUPS + 2)),
                dma((6,)),
                dma((6,)),
                dma((n_plane,)),
                dma((n_plane,)),
                dma((n_level,)),
                dma((n_level,)),
                pltpu.SemaphoreType.REGULAR,
                pltpu.SemaphoreType.REGULAR((3,)),
            ],
            compiler_params=pltpu.CompilerParams(collective_id=0, has_side_effects=True),
        )(perturbations, base_wind, base_height)
        return pl.pallas_call(
            functools.partial(finish, float(3 * 16 * n_lat * 128 * n_lon)),
            out_shape=(
                jax.ShapeDtypeStruct((MEMBERS, 3, 16, 128), jnp.float32),
                jax.ShapeDtypeStruct((MEMBERS, MEMBERS), jnp.float32),
            ),
            in_specs=[pl.BlockSpec(memory_space=pltpu.VMEM)] * 2,
            out_specs=(pl.BlockSpec(memory_space=pl.ANY), pl.BlockSpec(memory_space=pltpu.VMEM)),
            scratch_shapes=[
                pltpu.VMEM((16 * MEMBERS, 128), jnp.float32),
                pltpu.VMEM((MEMBERS, 3, 16, 128), jnp.float32),
                dma((MEMBERS,)),
            ],
        )(
            pltpu.with_memory_space_constraint(evolved, pltpu.VMEM),
            pltpu.with_memory_space_constraint(row, pltpu.VMEM),
        )

    return jax.shard_map(
        step,
        mesh=mesh,
        in_specs=(P(None, None, "lat", "lon"), P(None, "lat", "lon"), P("lat", "lon")),
        out_specs=(P(None, None, "lat", "lon"), P()),
        check_vma=False,
    )
```

```python
import functools
import math

import jax
import jax.numpy as jnp
from jax import lax
from jax.experimental import pallas as pl
from jax.experimental.pallas import tpu as pltpu
from jax.sharding import PartitionSpec as P

MEMBERS = 12
STEPS = 8
GROUP = 4
GROUPS = MEMBERS // GROUP
WIDTH = 8
EDGE = 24
STRIP = 32

advect_rate = 0.1
turn_rate = 0.5
gravity_rate = 0.2
diffuse_rate = 0.12

HALF = 0.5 * advect_rate
KEEP = 1.0 - 4.0 * diffuse_rate
PULL = 0.5 * gravity_rate
COEFS = 16


def roll(value, shift):
    shift = shift % 128
    return value if shift == 0 else pltpu.roll(value, shift, 1)


def lanes_of(rows):
    return lax.broadcasted_iota(jnp.int32, (rows, 128), 1)


def rows_of(rows):
    return lax.broadcasted_iota(jnp.int32, (rows, 128), 0)


def slot_of(local, var):
    return STRIP * local + WIDTH * var if local < GROUP else STRIP * var + EDGE


def kernel(
    n_lon,
    n_lat,
    x_hbm,
    wind_hbm,
    height_hbm,
    evolved,
    row_ref,
    ext,
    send_low,
    send_high,
    from_west,
    from_east,
    flow,
    base,
    coef,
    table,
    row_out,
    plane_in,
    column_in,
    turns,
    load_sem,
    lat_send,
    lat_recv,
    strip_send,
    strip_recv,
    plane_send,
    plane_recv,
    column_send,
    column_recv,
    plane_known,
    level_known,
):
    lon = lax.axis_index("lon")
    lat = lax.axis_index("lat")
    level = lon // 2
    core = lon % 2
    n_level = n_lon // 2
    n_plane = 2 * n_lat
    me_plane = lat * 2 + core
    east = (lon + 1) % n_lon
    west = (lon + n_lon - 1) % n_lon
    has_south = lat > 0
    has_north = lat < n_lat - 1

    def device(lon_index, lat_index):
        return {"lon": lon_index, "lat": lat_index}

    loads = [
        pltpu.make_async_copy(x_hbm, ext.at[0:MEMBERS, :, 8:24], load_sem.at[0]),
        pltpu.make_async_copy(wind_hbm, ext.at[MEMBERS, 0:2, 8:24], load_sem.at[1]),
        pltpu.make_async_copy(height_hbm, ext.at[MEMBERS, 2, 8:24], load_sem.at[2]),
    ]
    for load in loads:
        load.start()

    def plane_peer(step):
        index = me_plane ^ step
        return device(level * 2 + (index & 1), index >> 1)

    def column_peer(step):
        return device((level ^ step) * 2 + core, lat)

    def level_peer(step):
        return device(((level + step) & (n_level - 1)) * 2 + core, lat)

    barrier = pltpu.get_barrier_semaphore()
    across = jnp.where(core == 1, east, west)
    mate = lon ^ 1
    for there, row in ((has_south, lat - 1), (has_north, lat + 1)):

        @pl.when(there)
        def _():
            for column in (across, mate, lon):
                pl.semaphore_signal(barrier, inc=1, device_id=device(column, row))

    near = [level_peer(step) for step in (3, -3, 2, -2, 1, -1)] + [device(across, lat)]
    near += [plane_peer(step) for step in (16, 8, 24, 4, 5, 2, 3, 6, 7, 1)]
    for peer in near:
        pl.semaphore_signal(barrier, inc=1, device_id=peer)

    for tile in range(4):
        place = (lat * 16 - 8 + 8 * tile + rows_of(8)).astype(jnp.float32)
        turns[8 * tile : 8 * tile + 8, :] = turn_rate * jnp.sin(math.pi * ((place + 0.5) / (16 * n_lat) - 0.5))
    evolved[MEMBERS * 48 :, :] = jnp.zeros((4 * 48, 128), jnp.float32)
    def lat_copies(piece, north):
        rows = pl.ds(8, 8) if north else pl.ds(0, 8)
        place = pl.ds(0, 8) if north else pl.ds(24, 8)
        way = 0 if north else 1
        target = device(lon, lat + 1 if north else lat - 1)
        if piece == "wind":
            source, goal, sem = wind_hbm.at[:, rows], ext.at[MEMBERS, 0:2, place], GROUPS
        elif piece == "height":
            source, goal, sem = height_hbm.at[rows], ext.at[MEMBERS, 2, place], GROUPS + 1
        else:
            members = pl.ds(piece * GROUP, GROUP)
            source, goal, sem = x_hbm.at[members, :, rows], ext.at[members, :, place], piece
        return pltpu.make_async_remote_copy(
            src_ref=source,
            dst_ref=goal,
            send_sem=lat_send.at[way, sem],
            recv_sem=lat_recv.at[way, sem],
            device_id=target,
        )

    def strip_copy(to_east, shift):
        packed = send_high if to_east else send_low
        goal = from_west if to_east else from_east
        rows = {0: pl.ds(0, 16), 1: pl.ds(8, 8), -1: pl.ds(0, 8)}[shift]
        place = {0: pl.ds(8, 16), 1: pl.ds(0, 8), -1: pl.ds(24, 8)}[shift]
        sem = (0 if to_east else 3) + shift + 1
        return pltpu.make_async_remote_copy(
            src_ref=packed.at[:, rows],
            dst_ref=goal.at[:, place],
            send_sem=strip_send.at[sem],
            recv_sem=strip_recv.at[sem],
            device_id=device(east if to_east else west, lat + shift),
        )

    def when_sends(north, body):
        pl.when(has_north if north else has_south)(body)

    def when_receives(north, body):
        pl.when(has_south if north else has_north)(body)

    lane8 = lanes_of(8)

    for load in loads:
        load.wait()

    lane16 = lanes_of(16)

    @pl.loop(0, GROUPS)
    def _(group):
        low = jnp.zeros((16, 128), jnp.float32)
        high = jnp.zeros((16, 128), jnp.float32)
        for local in range(GROUP + 1):
            for var in range(3):
                value = ext[group * GROUP + local if local < GROUP else MEMBERS, var, pl.ds(8, 16)]
                slot = slot_of(local, var)
                inside = (lane16 >= slot) & (lane16 < slot + WIDTH)
                low = jnp.where(inside, roll(value, slot), low)
                high = jnp.where(inside, roll(value, slot - 120), high)
        send_low[group] = low
        send_high[group] = high

    pl.semaphore_wait(
        barrier,
        len(near) + 3 * (has_south.astype(jnp.int32) + has_north.astype(jnp.int32)),
    )
    for step in (8, 16, 24):
        pl.semaphore_signal(plane_known, inc=1, device_id=plane_peer(step))
    for step in (3, -3):
        pl.semaphore_signal(level_known.at[0], inc=1, device_id=level_peer(step))

    for to_east in (True, False):
        strip_copy(to_east, 0).start()
    for piece in ("wind", "height"):
        for north in (True, False):
            when_sends(north, lambda: lat_copies(piece, north).start())
    for to_east in (True, False):
        pl.when(has_north)(lambda: strip_copy(to_east, 1).start())
        pl.when(has_south)(lambda: strip_copy(to_east, -1).start())
    for piece in range(GROUPS):
        for north in (True, False):
            when_sends(north, lambda: lat_copies(piece, north).start())

    def present(tile, value):
        if tile == 0:
            return jnp.where(has_south, value, 0.0)
        if tile == 3:
            return jnp.where(has_north, value, 0.0)
        return value

    def rows_at(tile):
        return pl.ds(8 * tile, 8)

    def main_part(group, member, local, var, tile):
        rim = roll(from_west[group, rows_at(tile)], 128 - WIDTH - slot_of(local, var))
        return present(tile, jnp.where(lane8 < 128 - WIDTH, ext[member, var, rows_at(tile)], rim))

    def strip_own(total, member, var, place, tile):
        own = roll(ext[member, var, rows_at(tile)], STRIP * place + WIDTH - (128 - EDGE))
        return own if total is None else jnp.where((lane8 >= STRIP * place + WIDTH), own, total)

    def inside(start, value):
        row = rows_of(8) + start
        if start < 8:
            return jnp.where((row >= 8) | has_south, value, 0.0)
        if start > 16:
            return jnp.where((row < 24) | has_north, value, 0.0)
        return value

    def place_base(tile):
        rows = rows_at(tile)
        for var in range(3):
            base[0, var, rows] = main_part(0, MEMBERS, GROUP, var, tile)
            total = None
            for place in range(4):
                total = strip_own(total, MEMBERS, var, place, tile)
            for place in range(4):
                rim = roll(from_east[0, rows], STRIP * (place + 1) - slot_of(GROUP, var))
                first = STRIP * ((place + 1) % 4)
                total = jnp.where((lane8 >= first) & (lane8 < first + WIDTH), rim, total)
            base[1, var, rows] = present(tile, total)

    def place_members(group, tile):
        rows = rows_at(tile)
        for var in range(3):
            scale = PULL if var == 2 else 1.0
            total = None
            for local in range(GROUP):
                member = group * GROUP + local
                flow[group, 0, local, var, rows] = main_part(group, member, local, var, tile) * scale
                total = strip_own(total, member, var, local, tile)
            rim = roll(from_east[group, rows], STRIP - WIDTH * var)
            total = jnp.where(lane8 % STRIP < WIDTH, rim, total)
            flow[group, 0, GROUP, var, rows] = present(tile, total) * scale

    def rates(start):
        here, up, down = pl.ds(start, 8), pl.ds(start + 1, 8), pl.ds(start - 1, 8)
        turning = turns[start : start + 8, :]
        for kind in range(2):
            mean_x = base[kind, 0, here]
            mean_y = base[kind, 1, here]
            depth = base[kind, 2, here]
            x_up, x_down = base[kind, 0, up], base[kind, 0, down]
            y_up, y_down = base[kind, 1, up], base[kind, 1, down]
            x_east, x_west = roll(mean_x, -1), roll(mean_x, 1)
            values = [
                diffuse_rate - HALF * x_west,
                diffuse_rate + HALF * x_east,
                diffuse_rate - HALF * mean_x,
                diffuse_rate + HALF * mean_x,
                inside(start, diffuse_rate - HALF * mean_y),
                inside(start, diffuse_rate + HALF * mean_y),
                KEEP - HALF * (x_east - x_west),
                turning - HALF * (x_up - x_down),
                KEEP - HALF * (y_up - y_down),
                -turning - HALF * (roll(mean_y, -1) - roll(mean_y, 1)),
                (PULL * HALF) * depth,
                inside(start, diffuse_rate - HALF * y_up),
                inside(start, diffuse_rate + HALF * y_down),
                inside(start, (PULL * HALF) * base[kind, 2, up]),
                inside(start, (PULL * HALF) * base[kind, 2, down]),
                inside(start, jnp.ones((8, 128), jnp.float32)),
            ]
            for index, value in enumerate(values):
                coef[index, kind, here] = value

    def advance(group, source, target, starts):
        for start in starts:
            here, up, down = pl.ds(start, 8), pl.ds(start + 1, 8), pl.ds(start - 1, 8)
            inner = 8 <= start <= 16
            for kind, slots in ((0, range(GROUP)), (1, (GROUP,))):
                (e, w, e_h, w_h, n, s, keep_x, turn_x, keep_y, turn_y, deep, n_h, s_h, n_deep, s_deep) = [
                    coef[index, kind, pl.ds(start, 8)] for index in range(COEFS - 1)
                ]
                slope = None if inner else coef[COEFS - 1, kind, pl.ds(start, 8)]
                for slot in slots:
                    u, u_n, u_s = (flow[group, source, slot, 0, r] for r in (here, up, down))
                    v, v_n, v_s = (flow[group, source, slot, 1, r] for r in (here, up, down))
                    h, h_n, h_s = (flow[group, source, slot, 2, r] for r in (here, up, down))
                    carried = deep * u
                    flow[group, target, slot, 0, here] = (
                        (keep_x * u + turn_x * v)
                        + (n * u_n + s * u_s)
                        + (roll(e * u - h, -1) + roll(w * u + h, 1))
                    )
                    flow[group, target, slot, 1, here] = (
                        (keep_y * v + turn_y * u)
                        + (n * v_n + s * v_s)
                        + (roll(e * v, -1) + roll(w * v, 1))
                        - (h_n - h_s if inner else slope * (h_n - h_s))
                    )
                    flow[group, target, slot, 2, here] = (
                        KEEP * h
                        + (roll(e_h * h - carried, -1) + roll(w_h * h + carried, 1))
                        + (n_h * h_n + s_h * h_s)
                        - (n_deep * v_n - s_deep * v_s)
                    )

    for to_east in (True, False):
        strip_copy(to_east, 0).wait_recv()
    for tile in (1, 2):
        place_base(tile)
    for start in (9, 15):
        rates(start)

    @pl.loop(0, GROUPS)
    def _(group):
        for tile in (1, 2):
            place_members(group, tile)
        for index, starts in enumerate(((9, 15), (10, 14), (11, 13), (12,))):
            advance(group, index % 2, 1 - index % 2, starts)

    for piece in ("wind", "height"):
        for north in (True, False):
            when_receives(north, lambda: lat_copies(piece, north).wait_recv())
    for to_east in (True, False):
        pl.when(has_south)(lambda: strip_copy(to_east, 1).wait_recv())
        pl.when(has_north)(lambda: strip_copy(to_east, -1).wait_recv())
    for tile in (0, 3):
        place_base(tile)
    for start in (1, 23):
        rates(start)

    @pl.loop(0, GROUPS)
    def _(group):
        for north in (True, False):
            when_receives(north, lambda: lat_copies(group, north).wait_recv())
        for tile in (0, 3):
            place_members(group, tile)

        rest = ((1, 23), (2, 22), (3, 21), (4, 20), (5, 12, 19), (6, 12, 18), (7, 12, 17), (8, 16))
        for index, starts in enumerate(rest):
            advance(group, index % 2, 1 - index % 2, starts)
        for local in range(GROUP):
            for var in range(3):
                for tile in range(2):
                    rows = pl.ds(8 + 8 * tile, 8)
                    main = flow[group, 0, local, var, rows]
                    side = roll(flow[group, 0, GROUP, var, rows], 128 - STRIP * (local + 1))
                    at = pl.multiple_of((group * GROUP + local) * 48 + var * 16 + tile * 8, 8)
                    evolved[pl.ds(at, 8), :] = (
                        jnp.where(lane8 < 128 - 2 * WIDTH, main, side) * (1.0 / PULL if var == 2 else 1.0)
                    )

    pl.semaphore_wait(level_known.at[0], 2)
    for step in (4, -4):
        pl.semaphore_signal(level_known.at[1], inc=1, device_id=level_peer(step))

    flat = jnp.concatenate([evolved[pl.ds(j, 16, stride=48), :] for j in range(48)], axis=1)
    gram = lax.dot_general(
        flat,
        flat,
        (((1,), (1,)), ((), ())),
        precision=lax.Precision.HIGHEST,
        preferred_element_type=jnp.float32,
    )
    table[0:16, :] = jnp.zeros((16, 128), jnp.float32)
    table[0:16, 0:16] = gram
    row_id, lane = rows_of(16), lane16
    wide = table[0:16, :]
    wide = wide + roll(jnp.where((lane >= 8) & (lane < 12), wide, 0.0), 4)
    for shift in (16, 32, 64):
        wide = wide + roll(wide, shift)
    upper = (row_id < 8) & (lane // 16 == row_id) & (lane % 16 < 12)
    lower = (row_id >= 8) & (row_id < 12) & (lane // 16 == row_id - 8) & (lane % 16 >= 12)
    pick = upper | lower
    packed = jnp.sum(jnp.where(pick, wide, 0.0), axis=0, keepdims=True)

    def exchange_copy(slot, step, place):
        buffer, peer_of, send, recv = (
            (plane_in, plane_peer, plane_send, plane_recv),
            (column_in, column_peer, column_send, column_recv),
        )[slot]
        return pltpu.make_async_remote_copy(
            src_ref=row_out.at[slot],
            dst_ref=buffer.at[place],
            send_sem=send.at[step],
            recv_sem=recv.at[place],
            device_id=peer_of(step),
        )

    def exchange(value, slot, buffer, me, order, beside):
        row_out[slot] = value
        buffer[me] = value
        for step in order:
            exchange_copy(slot, step, me).start()
        beside()
        for step in reversed(order):
            exchange_copy(slot, step, me ^ step).wait_recv()
        parts = [buffer[index] for index in range(len(order) + 1)]
        while len(parts) > 1:
            parts = [a + b for a, b in zip(parts[0::2], parts[1::2])]
        return parts[0]

    def halo_sent():
        for piece in ("wind", "height", 0, 1, 2):
            for north in (True, False):
                when_sends(north, lambda: lat_copies(piece, north).wait_send())
        for to_east in (True, False):
            strip_copy(to_east, 0).wait_send()
            pl.when(has_north)(lambda: strip_copy(to_east, 1).wait_send())
            pl.when(has_south)(lambda: strip_copy(to_east, -1).wait_send())

    def plane_sent():
        for step in plane_order:
            exchange_copy(0, step, me_plane).wait_send()

    def hops(step):
        pair = {0: 0, 1: 1, 2: 2, 3: 1}
        return pair[(step >> 1) & 3] + pair[(step >> 3) & 3]

    plane_order = sorted(range(1, n_plane), key=lambda step: -hops(step))
    column_order = sorted(range(1, n_level), key=lambda step: -min(step, n_level - step))

    pl.semaphore_wait(plane_known, 3)
    packed = exchange(packed, 0, plane_in, me_plane, plane_order, halo_sent)
    pl.semaphore_wait(level_known.at[1], 2)
    packed = exchange(packed, 1, column_in, level, column_order, plane_sent)

    row_ref[...] = packed
    for step in column_order:
        exchange_copy(1, step, level).wait_send()


def finish(cells, evolved, row_ref, fields_hbm, factor_ref, table, out, sems):
    row_id, lane = rows_of(16), lanes_of(16)
    packed = row_ref[...]

    work = jnp.broadcast_to(packed / cells, (16, 128))
    for bit in range(3):
        work = jnp.where((row_id // (1 << bit)) % 2 == 1, roll(work, -(16 << bit)), work)
    work = jnp.where(row_id >= 8, roll(work, -4), work)
    turned = jnp.transpose(work)[0:16, :]
    table[0:16, 0:16] = turned
    turned = table[0:16, :]
    work = jnp.where((row_id >= 8) & (lane < 8), turned, work)
    work = jnp.where((lane < 12) & (row_id < 12), work, 0.0)
    left = [jnp.broadcast_to(work[:, k : k + 1], (16, 128)) for k in range(MEMBERS)]
    right = [jnp.where(row_id == k, 1.0, 0.0) for k in range(MEMBERS)]
    scales = []
    for k in range(MEMBERS):
        pivot = left[k][k : k + 1, :]
        scales.append(pivot)
        if k == MEMBERS - 1:
            break
        weight = jnp.where(row_id > k, left[k] * (1.0 / pivot), 0.0)
        for j in range(k + 1, MEMBERS):
            left[j] = left[j] - weight * left[j][k : k + 1, :]
        for j in range(k + 1):
            right[j] = right[j] - weight * right[j][k : k + 1, :]
    spread = jnp.ones((16, 128), jnp.float32)
    for k in range(MEMBERS):
        spread = jnp.where(row_id == k, scales[k], spread)
    spread = 1.0 / jnp.sqrt(spread)
    factor = jnp.zeros((16, 128), jnp.float32)
    for k in range(MEMBERS):
        factor = jnp.where((lane == k) & (row_id <= k), left[k], factor)
        table[16 * k : 16 * k + 16, :] = right[k] * spread
    factor_ref[...] = (factor * spread)[0:MEMBERS, 0:MEMBERS]

    def copy_out(member):
        return pltpu.make_async_copy(out.at[member], fields_hbm.at[member], sems.at[member])

    for m in range(MEMBERS):
        scale = [jnp.broadcast_to(table[16 * k + m : 16 * k + m + 1, :], (8, 128)) for k in range(m + 1)]
        for place in range(6):
            total = None
            for k in range(m + 1):
                term = scale[k] * evolved[48 * k + 8 * place : 48 * k + 8 * place + 8, :]
                total = term if total is None else total + term
            out[m, place // 2, 8 * (place % 2) : 8 * (place % 2) + 8, :] = total
        copy_out(m).start()
    for m in range(MEMBERS):
        copy_out(m).wait()


def solution(mesh):
    n_lon, n_lat = mesh.shape["lon"], mesh.shape["lat"]
    n_plane, n_level = 2 * n_lat, n_lon // 2
    dma = pltpu.SemaphoreType.DMA

    def step(perturbations, base_wind, base_height):
        evolved, row = pl.pallas_call(
            functools.partial(kernel, n_lon, n_lat),
            out_shape=(
                pltpu.VMEM((16 * 48, 128), jnp.float32),
                pltpu.VMEM((1, 128), jnp.float32),
            ),
            in_specs=[pl.BlockSpec(memory_space=pl.ANY)] * 3,
            out_specs=(pl.BlockSpec(memory_space=pltpu.VMEM), pl.BlockSpec(memory_space=pltpu.VMEM)),
            scratch_shapes=[
                pltpu.VMEM((MEMBERS + 1, 3, 32, 128), jnp.float32),
                pltpu.VMEM((GROUPS, 16, 128), jnp.float32),
                pltpu.VMEM((GROUPS, 16, 128), jnp.float32),
                pltpu.VMEM((GROUPS, 32, 128), jnp.float32),
                pltpu.VMEM((GROUPS, 32, 128), jnp.float32),
                pltpu.VMEM((GROUPS, 2, GROUP + 1, 3, 32, 128), jnp.float32),
                pltpu.VMEM((2, 3, 32, 128), jnp.float32),
                pltpu.VMEM((COEFS, 2, 32, 128), jnp.float32),
                pltpu.VMEM((16, 128), jnp.float32),
                pltpu.VMEM((2, 1, 128), jnp.float32),
                pltpu.VMEM((n_plane, 1, 128), jnp.float32),
                pltpu.VMEM((n_level, 1, 128), jnp.float32),
                pltpu.VMEM((32, 128), jnp.float32),
                dma((3,)),
                dma((2, GROUPS + 2)),
                dma((2, GROUPS + 2)),
                dma((6,)),
                dma((6,)),
                dma((n_plane,)),
                dma((n_plane,)),
                dma((n_level,)),
                dma((n_level,)),
                pltpu.SemaphoreType.REGULAR,
                pltpu.SemaphoreType.REGULAR((2,)),
            ],
            compiler_params=pltpu.CompilerParams(collective_id=0, has_side_effects=True),
        )(perturbations, base_wind, base_height)
        return pl.pallas_call(
            functools.partial(finish, float(3 * 16 * n_lat * 128 * n_lon)),
            out_shape=(
                jax.ShapeDtypeStruct((MEMBERS, 3, 16, 128), jnp.float32),
                jax.ShapeDtypeStruct((MEMBERS, MEMBERS), jnp.float32),
            ),
            in_specs=[pl.BlockSpec(memory_space=pltpu.VMEM)] * 2,
            out_specs=(pl.BlockSpec(memory_space=pl.ANY), pl.BlockSpec(memory_space=pltpu.VMEM)),
            scratch_shapes=[
                pltpu.VMEM((16 * MEMBERS, 128), jnp.float32),
                pltpu.VMEM((MEMBERS, 3, 16, 128), jnp.float32),
                dma((MEMBERS,)),
            ],
        )(
            pltpu.with_memory_space_constraint(evolved, pltpu.VMEM),
            pltpu.with_memory_space_constraint(row, pltpu.VMEM),
        )

    return jax.shard_map(
        step,
        mesh=mesh,
        in_specs=(P(None, None, "lat", "lon"), P(None, "lat", "lon"), P("lat", "lon")),
        out_specs=(P(None, None, "lat", "lon"), P()),
        check_vma=False,
    )
```

```python
import functools
import math

import jax
import jax.numpy as jnp
from jax import lax
from jax.experimental import pallas as pl
from jax.experimental.pallas import tpu as pltpu
from jax.sharding import PartitionSpec as P

MEMBERS = 12
STEPS = 8
GROUP = 4
GROUPS = MEMBERS // GROUP
WIDTH = 8
EDGE = 24
STRIP = 32

advect_rate = 0.1
turn_rate = 0.5
gravity_rate = 0.2
diffuse_rate = 0.12

HALF = 0.5 * advect_rate
KEEP = 1.0 - 4.0 * diffuse_rate
PULL = 0.5 * gravity_rate
COEFS = 16


def roll(value, shift):
    shift = shift % 128
    return value if shift == 0 else pltpu.roll(value, shift, 1)


def lanes_of(rows):
    return lax.broadcasted_iota(jnp.int32, (rows, 128), 1)


def rows_of(rows):
    return lax.broadcasted_iota(jnp.int32, (rows, 128), 0)


def slot_of(local, var):
    return STRIP * local + WIDTH * var if local < GROUP else STRIP * var + EDGE


def kernel(
    n_lon,
    n_lat,
    x_hbm,
    wind_hbm,
    height_hbm,
    evolved,
    row_ref,
    ext,
    send_low,
    send_high,
    from_west,
    from_east,
    flow,
    base,
    coef,
    table,
    row_out,
    plane_in,
    column_in,
    turns,
    load_sem,
    lat_send,
    lat_recv,
    strip_send,
    strip_recv,
    plane_send,
    plane_recv,
    column_send,
    column_recv,
    plane_known,
    level_known,
):
    lon = lax.axis_index("lon")
    lat = lax.axis_index("lat")
    level = lon // 2
    core = lon % 2
    n_level = n_lon // 2
    n_plane = 2 * n_lat
    me_plane = lat * 2 + core
    east = (lon + 1) % n_lon
    west = (lon + n_lon - 1) % n_lon
    has_south = lat > 0
    has_north = lat < n_lat - 1

    def device(lon_index, lat_index):
        return {"lon": lon_index, "lat": lat_index}

    loads = [
        pltpu.make_async_copy(x_hbm, ext.at[0:MEMBERS, :, 8:24], load_sem.at[0]),
        pltpu.make_async_copy(wind_hbm, ext.at[MEMBERS, 0:2, 8:24], load_sem.at[1]),
        pltpu.make_async_copy(height_hbm, ext.at[MEMBERS, 2, 8:24], load_sem.at[2]),
    ]
    for load in loads:
        load.start()

    def plane_peer(step):
        index = me_plane ^ step
        return device(level * 2 + (index & 1), index >> 1)

    def column_peer(step):
        return device((level ^ step) * 2 + core, lat)

    def level_peer(step):
        return device(((level + step) & (n_level - 1)) * 2 + core, lat)

    barrier = pltpu.get_barrier_semaphore()
    across = jnp.where(core == 1, east, west)
    mate = lon ^ 1
    for there, row in ((has_south, lat - 1), (has_north, lat + 1)):

        @pl.when(there)
        def _():
            for column in (across, mate, lon):
                pl.semaphore_signal(barrier, inc=1, device_id=device(column, row))

    near = [level_peer(step) for step in (3, -3, 2, -2, 1, -1)] + [device(across, lat)]
    near += [plane_peer(step) for step in (16, 8, 24, 4, 5, 2, 3, 6, 7, 1)]
    for peer in near:
        pl.semaphore_signal(barrier, inc=1, device_id=peer)

    for tile in range(4):
        place = (lat * 16 - 8 + 8 * tile + rows_of(8)).astype(jnp.float32)
        turns[8 * tile : 8 * tile + 8, :] = turn_rate * jnp.sin(math.pi * ((place + 0.5) / (16 * n_lat) - 0.5))
    evolved[MEMBERS * 48 :, :] = jnp.zeros((4 * 48, 128), jnp.float32)
    def lat_copies(piece, north):
        rows = pl.ds(8, 8) if north else pl.ds(0, 8)
        place = pl.ds(0, 8) if north else pl.ds(24, 8)
        way = 0 if north else 1
        target = device(lon, lat + 1 if north else lat - 1)
        if piece == "wind":
            source, goal, sem = wind_hbm.at[:, rows], ext.at[MEMBERS, 0:2, place], GROUPS
        elif piece == "height":
            source, goal, sem = height_hbm.at[rows], ext.at[MEMBERS, 2, place], GROUPS + 1
        else:
            members = pl.ds(piece * GROUP, GROUP)
            source, goal, sem = x_hbm.at[members, :, rows], ext.at[members, :, place], piece
        return pltpu.make_async_remote_copy(
            src_ref=source,
            dst_ref=goal,
            send_sem=lat_send.at[way, sem],
            recv_sem=lat_recv.at[way, sem],
            device_id=target,
        )

    def strip_copy(to_east, shift):
        packed = send_high if to_east else send_low
        goal = from_west if to_east else from_east
        rows = {0: pl.ds(0, 16), 1: pl.ds(8, 8), -1: pl.ds(0, 8)}[shift]
        place = {0: pl.ds(8, 16), 1: pl.ds(0, 8), -1: pl.ds(24, 8)}[shift]
        sem = (0 if to_east else 3) + shift + 1
        return pltpu.make_async_remote_copy(
            src_ref=packed.at[:, rows],
            dst_ref=goal.at[:, place],
            send_sem=strip_send.at[sem],
            recv_sem=strip_recv.at[sem],
            device_id=device(east if to_east else west, lat + shift),
        )

    def when_sends(north, body):
        pl.when(has_north if north else has_south)(body)

    def when_receives(north, body):
        pl.when(has_south if north else has_north)(body)

    lane8 = lanes_of(8)

    for load in loads:
        load.wait()

    lane16 = lanes_of(16)

    @pl.loop(0, GROUPS)
    def _(group):
        low = jnp.zeros((16, 128), jnp.float32)
        high = jnp.zeros((16, 128), jnp.float32)
        for local in range(GROUP + 1):
            for var in range(3):
                value = ext[group * GROUP + local if local < GROUP else MEMBERS, var, pl.ds(8, 16)]
                slot = slot_of(local, var)
                inside = (lane16 >= slot) & (lane16 < slot + WIDTH)
                low = jnp.where(inside, roll(value, slot), low)
                high = jnp.where(inside, roll(value, slot - 120), high)
        send_low[group] = low
        send_high[group] = high

    pl.semaphore_wait(
        barrier,
        len(near) + 3 * (has_south.astype(jnp.int32) + has_north.astype(jnp.int32)),
    )
    for step in (8, 16, 24):
        pl.semaphore_signal(plane_known, inc=1, device_id=plane_peer(step))
    for step in (3, -3):
        pl.semaphore_signal(level_known.at[0], inc=1, device_id=level_peer(step))

    for to_east in (True, False):
        strip_copy(to_east, 0).start()
    for piece in ("wind", "height"):
        for north in (True, False):
            when_sends(north, lambda: lat_copies(piece, north).start())
    for to_east in (True, False):
        pl.when(has_north)(lambda: strip_copy(to_east, 1).start())
        pl.when(has_south)(lambda: strip_copy(to_east, -1).start())
    for piece in range(GROUPS):
        for north in (True, False):
            when_sends(north, lambda: lat_copies(piece, north).start())

    def present(tile, value):
        if tile == 0:
            return jnp.where(has_south, value, 0.0)
        if tile == 3:
            return jnp.where(has_north, value, 0.0)
        return value

    def rows_at(tile):
        return pl.ds(8 * tile, 8)

    def main_part(group, member, local, var, tile):
        rim = roll(from_west[group, rows_at(tile)], 128 - WIDTH - slot_of(local, var))
        return present(tile, jnp.where(lane8 < 128 - WIDTH, ext[member, var, rows_at(tile)], rim))

    def strip_own(total, member, var, place, tile):
        own = roll(ext[member, var, rows_at(tile)], STRIP * place + WIDTH - (128 - EDGE))
        return own if total is None else jnp.where((lane8 >= STRIP * place + WIDTH), own, total)

    def inside(start, value):
        row = rows_of(8) + start
        if start < 8:
            return jnp.where((row >= 8) | has_south, value, 0.0)
        if start > 16:
            return jnp.where((row < 24) | has_north, value, 0.0)
        return value

    def place_base(tile):
        rows = rows_at(tile)
        for var in range(3):
            base[0, var, rows] = main_part(0, MEMBERS, GROUP, var, tile)
            total = None
            for place in range(4):
                total = strip_own(total, MEMBERS, var, place, tile)
            for place in range(4):
                rim = roll(from_east[0, rows], STRIP * (place + 1) - slot_of(GROUP, var))
                first = STRIP * ((place + 1) % 4)
                total = jnp.where((lane8 >= first) & (lane8 < first + WIDTH), rim, total)
            base[1, var, rows] = present(tile, total)

    def place_members(group, tile):
        rows = rows_at(tile)
        for var in range(3):
            scale = PULL if var == 2 else 1.0
            total = None
            for local in range(GROUP):
                member = group * GROUP + local
                flow[group, 0, local, var, rows] = main_part(group, member, local, var, tile) * scale
                total = strip_own(total, member, var, local, tile)
            rim = roll(from_east[group, rows], STRIP - WIDTH * var)
            total = jnp.where(lane8 % STRIP < WIDTH, rim, total)
            flow[group, 0, GROUP, var, rows] = present(tile, total) * scale

    def rates(start):
        here, up, down = pl.ds(start, 8), pl.ds(start + 1, 8), pl.ds(start - 1, 8)
        turning = turns[start : start + 8, :]
        for kind in range(2):
            mean_x = base[kind, 0, here]
            mean_y = base[kind, 1, here]
            depth = base[kind, 2, here]
            x_up, x_down = base[kind, 0, up], base[kind, 0, down]
            y_up, y_down = base[kind, 1, up], base[kind, 1, down]
            x_east, x_west = roll(mean_x, -1), roll(mean_x, 1)
            values = [
                diffuse_rate - HALF * x_west,
                diffuse_rate + HALF * x_east,
                diffuse_rate - HALF * mean_x,
                diffuse_rate + HALF * mean_x,
                inside(start, diffuse_rate - HALF * mean_y),
                inside(start, diffuse_rate + HALF * mean_y),
                KEEP - HALF * (x_east - x_west),
                turning - HALF * (x_up - x_down),
                KEEP - HALF * (y_up - y_down),
                -turning - HALF * (roll(mean_y, -1) - roll(mean_y, 1)),
                (PULL * HALF) * depth,
                inside(start, diffuse_rate - HALF * y_up),
                inside(start, diffuse_rate + HALF * y_down),
                inside(start, (PULL * HALF) * base[kind, 2, up]),
                inside(start, (PULL * HALF) * base[kind, 2, down]),
                inside(start, jnp.ones((8, 128), jnp.float32)),
            ]
            for index, value in enumerate(values):
                coef[index, kind, here] = value

    def advance(group, source, target, starts):
        for start in starts:
            here, up, down = pl.ds(start, 8), pl.ds(start + 1, 8), pl.ds(start - 1, 8)
            inner = 8 <= start <= 16
            for kind, slots in ((0, range(GROUP)), (1, (GROUP,))):
                (e, w, e_h, w_h, n, s, keep_x, turn_x, keep_y, turn_y, deep, n_h, s_h, n_deep, s_deep) = [
                    coef[index, kind, pl.ds(start, 8)] for index in range(COEFS - 1)
                ]
                slope = None if inner else coef[COEFS - 1, kind, pl.ds(start, 8)]
                for slot in slots:
                    u, u_n, u_s = (flow[group, source, slot, 0, r] for r in (here, up, down))
                    v, v_n, v_s = (flow[group, source, slot, 1, r] for r in (here, up, down))
                    h, h_n, h_s = (flow[group, source, slot, 2, r] for r in (here, up, down))
                    carried = deep * u
                    flow[group, target, slot, 0, here] = (
                        (keep_x * u + turn_x * v)
                        + (n * u_n + s * u_s)
                        + (roll(e * u - h, -1) + roll(w * u + h, 1))
                    )
                    flow[group, target, slot, 1, here] = (
                        (keep_y * v + turn_y * u)
                        + (n * v_n + s * v_s)
                        + (roll(e * v, -1) + roll(w * v, 1))
                        - (h_n - h_s if inner else slope * (h_n - h_s))
                    )
                    flow[group, target, slot, 2, here] = (
                        KEEP * h
                        + (roll(e_h * h - carried, -1) + roll(w_h * h + carried, 1))
                        + (n_h * h_n + s_h * h_s)
                        - (n_deep * v_n - s_deep * v_s)
                    )

    for to_east in (True, False):
        strip_copy(to_east, 0).wait_recv()
    for tile in (1, 2):
        place_base(tile)
    for start in (9, 15):
        rates(start)

    @pl.loop(0, GROUPS)
    def _(group):
        for tile in (1, 2):
            place_members(group, tile)
        for index, starts in enumerate(((9, 15), (10, 14), (11, 13), (12,))):
            advance(group, index % 2, 1 - index % 2, starts)

    for piece in ("wind", "height"):
        for north in (True, False):
            when_receives(north, lambda: lat_copies(piece, north).wait_recv())
    for to_east in (True, False):
        pl.when(has_south)(lambda: strip_copy(to_east, 1).wait_recv())
        pl.when(has_north)(lambda: strip_copy(to_east, -1).wait_recv())
    for tile in (0, 3):
        place_base(tile)
    for start in (1, 23):
        rates(start)

    @pl.loop(0, GROUPS)
    def _(group):
        for north in (True, False):
            when_receives(north, lambda: lat_copies(group, north).wait_recv())
        for tile in (0, 3):
            place_members(group, tile)

        rest = ((1, 23), (2, 22), (3, 21), (4, 20), (5, 12, 19), (6, 12, 18), (7, 12, 17), (8, 16))
        for index, starts in enumerate(rest):
            advance(group, index % 2, 1 - index % 2, starts)
        for local in range(GROUP):
            for var in range(3):
                for tile in range(2):
                    rows = pl.ds(8 + 8 * tile, 8)
                    main = flow[group, 0, local, var, rows]
                    side = roll(flow[group, 0, GROUP, var, rows], 128 - STRIP * (local + 1))
                    at = pl.multiple_of((group * GROUP + local) * 48 + var * 16 + tile * 8, 8)
                    evolved[pl.ds(at, 8), :] = (
                        jnp.where(lane8 < 128 - 2 * WIDTH, main, side) * (1.0 / PULL if var == 2 else 1.0)
                    )

    pl.semaphore_wait(level_known.at[0], 2)
    for step in (4, -4):
        pl.semaphore_signal(level_known.at[1], inc=1, device_id=level_peer(step))

    flat = jnp.concatenate([evolved[pl.ds(j, 16, stride=48), :] for j in range(48)], axis=1)
    gram = lax.dot_general(
        flat,
        flat,
        (((1,), (1,)), ((), ())),
        precision=lax.Precision.HIGHEST,
        preferred_element_type=jnp.float32,
    )
    table[0:16, :] = jnp.zeros((16, 128), jnp.float32)
    table[0:16, 0:16] = gram
    row_id, lane = rows_of(16), lane16
    wide = table[0:16, :]
    wide = wide + roll(jnp.where((lane >= 8) & (lane < 12), wide, 0.0), 4)
    for shift in (16, 32, 64):
        wide = wide + roll(wide, shift)
    upper = (row_id < 8) & (lane // 16 == row_id) & (lane % 16 < 12)
    lower = (row_id >= 8) & (row_id < 12) & (lane // 16 == row_id - 8) & (lane % 16 >= 12)
    pick = upper | lower
    packed = jnp.sum(jnp.where(pick, wide, 0.0), axis=0, keepdims=True)

    def exchange_copy(slot, step, place):
        buffer, peer_of, send, recv = (
            (plane_in, plane_peer, plane_send, plane_recv),
            (column_in, column_peer, column_send, column_recv),
        )[slot]
        return pltpu.make_async_remote_copy(
            src_ref=row_out.at[slot],
            dst_ref=buffer.at[place],
            send_sem=send.at[step],
            recv_sem=recv.at[place],
            device_id=peer_of(step),
        )

    def exchange(value, slot, buffer, me, order, beside):
        row_out[slot] = value
        buffer[me] = value
        for step in order:
            exchange_copy(slot, step, me).start()
        beside()
        for step in reversed(order):
            exchange_copy(slot, step, me ^ step).wait_recv()
        parts = [buffer[index] for index in range(len(order) + 1)]
        while len(parts) > 1:
            parts = [a + b for a, b in zip(parts[0::2], parts[1::2])]
        return parts[0]

    def halo_sent():
        for piece in ("wind", "height", 0, 1, 2):
            for north in (True, False):
                when_sends(north, lambda: lat_copies(piece, north).wait_send())
        for to_east in (True, False):
            strip_copy(to_east, 0).wait_send()
            pl.when(has_north)(lambda: strip_copy(to_east, 1).wait_send())
            pl.when(has_south)(lambda: strip_copy(to_east, -1).wait_send())

    def plane_sent():
        for step in plane_order:
            exchange_copy(0, step, me_plane).wait_send()

    def hops(step):
        pair = {0: 0, 1: 1, 2: 2, 3: 1}
        return pair[(step >> 1) & 3] + pair[(step >> 3) & 3]

    plane_order = sorted(range(1, n_plane), key=lambda step: -hops(step))
    column_order = sorted(range(1, n_level), key=lambda step: -min(step, n_level - step))

    pl.semaphore_wait(plane_known, 3)
    packed = exchange(packed, 0, plane_in, me_plane, plane_order, halo_sent)
    pl.semaphore_wait(level_known.at[1], 2)
    packed = exchange(packed, 1, column_in, level, column_order, plane_sent)

    row_ref[...] = packed
    for step in column_order:
        exchange_copy(1, step, level).wait_send()


def finish(cells, evolved, row_ref, fields_hbm, factor_hbm, table, out, factor_ref, sems):
    row_id, lane = rows_of(16), lanes_of(16)
    packed = row_ref[...]

    work = jnp.broadcast_to(packed / cells, (16, 128))
    for bit in range(3):
        work = jnp.where((row_id // (1 << bit)) % 2 == 1, roll(work, -(16 << bit)), work)
    work = jnp.where(row_id >= 8, roll(work, -4), work)
    turned = jnp.transpose(work)[0:16, :]
    table[0:16, 0:16] = turned
    turned = table[0:16, :]
    work = jnp.where((row_id >= 8) & (lane < 8), turned, work)
    work = jnp.where((lane < 12) & (row_id < 12), work, 0.0)
    left = [jnp.broadcast_to(work[:, k : k + 1], (16, 128)) for k in range(MEMBERS)]
    right = [jnp.where(row_id == k, 1.0, 0.0) for k in range(MEMBERS)]
    scales = []
    for k in range(MEMBERS):
        pivot = left[k][k : k + 1, :]
        scales.append(pivot)
        if k == MEMBERS - 1:
            break
        weight = jnp.where(row_id > k, left[k] * (1.0 / pivot), 0.0)
        for j in range(k + 1, MEMBERS):
            left[j] = left[j] - weight * left[j][k : k + 1, :]
        for j in range(k + 1):
            right[j] = right[j] - weight * right[j][k : k + 1, :]
    spread = jnp.ones((16, 128), jnp.float32)
    for k in range(MEMBERS):
        spread = jnp.where(row_id == k, scales[k], spread)
    spread = 1.0 / jnp.sqrt(spread)
    factor = jnp.zeros((16, 128), jnp.float32)
    for k in range(MEMBERS):
        factor = jnp.where((lane == k) & (row_id <= k), left[k], factor)
        table[16 * k : 16 * k + 16, :] = right[k] * spread
    factor_ref[...] = (factor * spread)[0:MEMBERS, 0:MEMBERS]
    factor_out = pltpu.make_async_copy(factor_ref, factor_hbm, sems.at[MEMBERS])
    factor_out.start()

    def copy_out(member):
        return pltpu.make_async_copy(out.at[member], fields_hbm.at[member], sems.at[member])

    for m in range(MEMBERS):
        scale = [jnp.broadcast_to(table[16 * k + m : 16 * k + m + 1, :], (8, 128)) for k in range(m + 1)]
        for place in range(6):
            total = None
            for k in range(m + 1):
                term = scale[k] * evolved[48 * k + 8 * place : 48 * k + 8 * place + 8, :]
                total = term if total is None else total + term
            out[m, place // 2, 8 * (place % 2) : 8 * (place % 2) + 8, :] = total
        copy_out(m).start()
    factor_out.wait()
    for m in range(MEMBERS):
        copy_out(m).wait()


def solution(mesh):
    n_lon, n_lat = mesh.shape["lon"], mesh.shape["lat"]
    n_plane, n_level = 2 * n_lat, n_lon // 2
    dma = pltpu.SemaphoreType.DMA

    def step(perturbations, base_wind, base_height):
        evolved, row = pl.pallas_call(
            functools.partial(kernel, n_lon, n_lat),
            out_shape=(
                pltpu.VMEM((16 * 48, 128), jnp.float32),
                pltpu.VMEM((1, 128), jnp.float32),
            ),
            in_specs=[pl.BlockSpec(memory_space=pl.ANY)] * 3,
            out_specs=(pl.BlockSpec(memory_space=pltpu.VMEM), pl.BlockSpec(memory_space=pltpu.VMEM)),
            scratch_shapes=[
                pltpu.VMEM((MEMBERS + 1, 3, 32, 128), jnp.float32),
                pltpu.VMEM((GROUPS, 16, 128), jnp.float32),
                pltpu.VMEM((GROUPS, 16, 128), jnp.float32),
                pltpu.VMEM((GROUPS, 32, 128), jnp.float32),
                pltpu.VMEM((GROUPS, 32, 128), jnp.float32),
                pltpu.VMEM((GROUPS, 2, GROUP + 1, 3, 32, 128), jnp.float32),
                pltpu.VMEM((2, 3, 32, 128), jnp.float32),
                pltpu.VMEM((COEFS, 2, 32, 128), jnp.float32),
                pltpu.VMEM((16, 128), jnp.float32),
                pltpu.VMEM((2, 1, 128), jnp.float32),
                pltpu.VMEM((n_plane, 1, 128), jnp.float32),
                pltpu.VMEM((n_level, 1, 128), jnp.float32),
                pltpu.VMEM((32, 128), jnp.float32),
                dma((3,)),
                dma((2, GROUPS + 2)),
                dma((2, GROUPS + 2)),
                dma((6,)),
                dma((6,)),
                dma((n_plane,)),
                dma((n_plane,)),
                dma((n_level,)),
                dma((n_level,)),
                pltpu.SemaphoreType.REGULAR,
                pltpu.SemaphoreType.REGULAR((2,)),
            ],
            compiler_params=pltpu.CompilerParams(collective_id=0, has_side_effects=True),
        )(perturbations, base_wind, base_height)
        return pl.pallas_call(
            functools.partial(finish, float(3 * 16 * n_lat * 128 * n_lon)),
            out_shape=(
                jax.ShapeDtypeStruct((MEMBERS, 3, 16, 128), jnp.float32),
                jax.ShapeDtypeStruct((MEMBERS, MEMBERS), jnp.float32),
            ),
            in_specs=[pl.BlockSpec(memory_space=pltpu.VMEM)] * 2,
            out_specs=(pl.BlockSpec(memory_space=pl.ANY), pl.BlockSpec(memory_space=pl.ANY)),
            scratch_shapes=[
                pltpu.VMEM((16 * MEMBERS, 128), jnp.float32),
                pltpu.VMEM((MEMBERS, 3, 16, 128), jnp.float32),
                pltpu.VMEM((MEMBERS, MEMBERS), jnp.float32),
                dma((MEMBERS + 1,)),
            ],
        )(
            pltpu.with_memory_space_constraint(evolved, pltpu.VMEM),
            pltpu.with_memory_space_constraint(row, pltpu.VMEM),
        )

    return jax.shard_map(
        step,
        mesh=mesh,
        in_specs=(P(None, None, "lat", "lon"), P(None, "lat", "lon"), P("lat", "lon")),
        out_specs=(P(None, None, "lat", "lon"), P()),
        check_vma=False,
    )
```

```python
import functools
import math

import jax
import jax.numpy as jnp
from jax import lax
from jax.experimental import pallas as pl
from jax.experimental.pallas import tpu as pltpu
from jax.sharding import PartitionSpec as P

MEMBERS = 12
STEPS = 8
GROUP = 4
GROUPS = MEMBERS // GROUP
WIDTH = 8
EDGE = 24
STRIP = 32

advect_rate = 0.1
turn_rate = 0.5
gravity_rate = 0.2
diffuse_rate = 0.12

HALF = 0.5 * advect_rate
KEEP = 1.0 - 4.0 * diffuse_rate
PULL = 0.5 * gravity_rate
COEFS = 16


def roll(value, shift):
    shift = shift % 128
    return value if shift == 0 else pltpu.roll(value, shift, 1)


def lanes_of(rows):
    return lax.broadcasted_iota(jnp.int32, (rows, 128), 1)


def rows_of(rows):
    return lax.broadcasted_iota(jnp.int32, (rows, 128), 0)


def slot_of(local, var):
    return STRIP * local + WIDTH * var if local < GROUP else STRIP * var + EDGE


def kernel(
    n_lon,
    n_lat,
    x_hbm,
    wind_hbm,
    height_hbm,
    evolved,
    row_ref,
    ext,
    send_low,
    send_high,
    from_west,
    from_east,
    flow,
    base,
    coef,
    table,
    row_out,
    plane_in,
    column_in,
    turns,
    load_sem,
    lat_send,
    lat_recv,
    strip_send,
    strip_recv,
    plane_send,
    plane_recv,
    column_send,
    column_recv,
    plane_known,
    level_known,
):
    lon = lax.axis_index("lon")
    lat = lax.axis_index("lat")
    level = lon // 2
    core = lon % 2
    n_level = n_lon // 2
    n_plane = 2 * n_lat
    me_plane = lat * 2 + core
    east = (lon + 1) % n_lon
    west = (lon + n_lon - 1) % n_lon
    has_south = lat > 0
    has_north = lat < n_lat - 1

    def device(lon_index, lat_index):
        return {"lon": lon_index, "lat": lat_index}

    loads = [
        pltpu.make_async_copy(x_hbm, ext.at[0:MEMBERS, :, 8:24], load_sem.at[0]),
        pltpu.make_async_copy(wind_hbm, ext.at[MEMBERS, 0:2, 8:24], load_sem.at[1]),
        pltpu.make_async_copy(height_hbm, ext.at[MEMBERS, 2, 8:24], load_sem.at[2]),
    ]
    for load in loads:
        load.start()

    def plane_peer(step):
        index = me_plane ^ step
        return device(level * 2 + (index & 1), index >> 1)

    def column_peer(step):
        return device((level ^ step) * 2 + core, lat)

    def level_peer(step):
        return device(((level + step) & (n_level - 1)) * 2 + core, lat)

    barrier = pltpu.get_barrier_semaphore()
    across = jnp.where(core == 1, east, west)
    mate = lon ^ 1
    for there, row in ((has_south, lat - 1), (has_north, lat + 1)):

        @pl.when(there)
        def _():
            for column in (across, mate, lon):
                pl.semaphore_signal(barrier, inc=1, device_id=device(column, row))

    near = [level_peer(step) for step in (3, -3, 2, -2, 1, -1)] + [device(across, lat)]
    near += [plane_peer(step) for step in (16, 8, 24, 4, 5, 2, 3, 6, 7, 1)]
    for peer in near:
        pl.semaphore_signal(barrier, inc=1, device_id=peer)

    for tile in range(4):
        place = (lat * 16 - 8 + 8 * tile + rows_of(8)).astype(jnp.float32)
        turns[8 * tile : 8 * tile + 8, :] = turn_rate * jnp.sin(math.pi * ((place + 0.5) / (16 * n_lat) - 0.5))
    evolved[MEMBERS * 48 :, :] = jnp.zeros((4 * 48, 128), jnp.float32)
    def lat_copies(piece, north):
        rows = pl.ds(8, 8) if north else pl.ds(0, 8)
        place = pl.ds(0, 8) if north else pl.ds(24, 8)
        way = 0 if north else 1
        target = device(lon, lat + 1 if north else lat - 1)
        if piece == "wind":
            source, goal, sem = wind_hbm.at[:, rows], ext.at[MEMBERS, 0:2, place], GROUPS
        elif piece == "height":
            source, goal, sem = height_hbm.at[rows], ext.at[MEMBERS, 2, place], GROUPS + 1
        else:
            members = pl.ds(piece * GROUP, GROUP)
            source, goal, sem = x_hbm.at[members, :, rows], ext.at[members, :, place], piece
        return pltpu.make_async_remote_copy(
            src_ref=source,
            dst_ref=goal,
            send_sem=lat_send.at[way, sem],
            recv_sem=lat_recv.at[way, sem],
            device_id=target,
        )

    def strip_copy(to_east, shift):
        packed = send_high if to_east else send_low
        goal = from_west if to_east else from_east
        rows = {0: pl.ds(0, 16), 1: pl.ds(8, 8), -1: pl.ds(0, 8)}[shift]
        place = {0: pl.ds(8, 16), 1: pl.ds(0, 8), -1: pl.ds(24, 8)}[shift]
        sem = (0 if to_east else 3) + shift + 1
        return pltpu.make_async_remote_copy(
            src_ref=packed.at[:, rows],
            dst_ref=goal.at[:, place],
            send_sem=strip_send.at[sem],
            recv_sem=strip_recv.at[sem],
            device_id=device(east if to_east else west, lat + shift),
        )

    def when_sends(north, body):
        pl.when(has_north if north else has_south)(body)

    def when_receives(north, body):
        pl.when(has_south if north else has_north)(body)

    lane8 = lanes_of(8)

    for load in loads:
        load.wait()

    lane16 = lanes_of(16)

    @pl.loop(0, GROUPS)
    def _(group):
        low = jnp.zeros((16, 128), jnp.float32)
        high = jnp.zeros((16, 128), jnp.float32)
        for local in range(GROUP + 1):
            for var in range(3):
                value = ext[group * GROUP + local if local < GROUP else MEMBERS, var, pl.ds(8, 16)]
                slot = slot_of(local, var)
                inside = (lane16 >= slot) & (lane16 < slot + WIDTH)
                low = jnp.where(inside, roll(value, slot), low)
                high = jnp.where(inside, roll(value, slot - 120), high)
        send_low[group] = low
        send_high[group] = high

    pl.semaphore_wait(
        barrier,
        len(near) + 3 * (has_south.astype(jnp.int32) + has_north.astype(jnp.int32)),
    )
    for step in (8, 16, 24):
        pl.semaphore_signal(plane_known, inc=1, device_id=plane_peer(step))
    for step in (3, -3):
        pl.semaphore_signal(level_known.at[0], inc=1, device_id=level_peer(step))

    for to_east in (True, False):
        strip_copy(to_east, 0).start()
    for piece in ("wind", "height"):
        for north in (True, False):
            when_sends(north, lambda: lat_copies(piece, north).start())
    for to_east in (True, False):
        pl.when(has_north)(lambda: strip_copy(to_east, 1).start())
        pl.when(has_south)(lambda: strip_copy(to_east, -1).start())
    for piece in range(GROUPS):
        for north in (True, False):
            when_sends(north, lambda: lat_copies(piece, north).start())

    def present(tile, value):
        if tile == 0:
            return jnp.where(has_south, value, 0.0)
        if tile == 3:
            return jnp.where(has_north, value, 0.0)
        return value

    def rows_at(tile):
        return pl.ds(8 * tile, 8)

    def main_part(group, member, local, var, tile):
        rim = roll(from_west[group, rows_at(tile)], 128 - WIDTH - slot_of(local, var))
        return present(tile, jnp.where(lane8 < 128 - WIDTH, ext[member, var, rows_at(tile)], rim))

    def strip_own(total, member, var, place, tile):
        own = roll(ext[member, var, rows_at(tile)], STRIP * place + WIDTH - (128 - EDGE))
        return own if total is None else jnp.where((lane8 >= STRIP * place + WIDTH), own, total)

    def inside(start, value):
        row = rows_of(8) + start
        if start < 8:
            return jnp.where((row >= 8) | has_south, value, 0.0)
        if start > 16:
            return jnp.where((row < 24) | has_north, value, 0.0)
        return value

    def place_base(tile):
        rows = rows_at(tile)
        for var in range(3):
            base[0, var, rows] = main_part(0, MEMBERS, GROUP, var, tile)
            total = None
            for place in range(4):
                total = strip_own(total, MEMBERS, var, place, tile)
            for place in range(4):
                rim = roll(from_east[0, rows], STRIP * (place + 1) - slot_of(GROUP, var))
                first = STRIP * ((place + 1) % 4)
                total = jnp.where((lane8 >= first) & (lane8 < first + WIDTH), rim, total)
            base[1, var, rows] = present(tile, total)

    def place_members(group, tile):
        rows = rows_at(tile)
        for var in range(3):
            scale = PULL if var == 2 else 1.0
            total = None
            for local in range(GROUP):
                member = group * GROUP + local
                flow[group, 0, local, var, rows] = main_part(group, member, local, var, tile) * scale
                total = strip_own(total, member, var, local, tile)
            rim = roll(from_east[group, rows], STRIP - WIDTH * var)
            total = jnp.where(lane8 % STRIP < WIDTH, rim, total)
            flow[group, 0, GROUP, var, rows] = present(tile, total) * scale

    def rates(start):
        here, up, down = pl.ds(start, 8), pl.ds(start + 1, 8), pl.ds(start - 1, 8)
        turning = turns[start : start + 8, :]
        for kind in range(2):
            mean_x = base[kind, 0, here]
            mean_y = base[kind, 1, here]
            depth = base[kind, 2, here]
            x_up, x_down = base[kind, 0, up], base[kind, 0, down]
            y_up, y_down = base[kind, 1, up], base[kind, 1, down]
            x_east, x_west = roll(mean_x, -1), roll(mean_x, 1)
            values = [
                diffuse_rate - HALF * x_west,
                diffuse_rate + HALF * x_east,
                diffuse_rate - HALF * mean_x,
                diffuse_rate + HALF * mean_x,
                inside(start, diffuse_rate - HALF * mean_y),
                inside(start, diffuse_rate + HALF * mean_y),
                KEEP - HALF * (x_east - x_west),
                turning - HALF * (x_up - x_down),
                KEEP - HALF * (y_up - y_down),
                -turning - HALF * (roll(mean_y, -1) - roll(mean_y, 1)),
                (PULL * HALF) * depth,
                inside(start, diffuse_rate - HALF * y_up),
                inside(start, diffuse_rate + HALF * y_down),
                inside(start, (PULL * HALF) * base[kind, 2, up]),
                inside(start, (PULL * HALF) * base[kind, 2, down]),
                inside(start, jnp.ones((8, 128), jnp.float32)),
            ]
            for index, value in enumerate(values):
                coef[index, kind, here] = value

    def advance(group, source, target, starts):
        for start in starts:
            here, up, down = pl.ds(start, 8), pl.ds(start + 1, 8), pl.ds(start - 1, 8)
            inner = 8 <= start <= 16
            for kind, slots in ((0, range(GROUP)), (1, (GROUP,))):
                (e, w, e_h, w_h, n, s, keep_x, turn_x, keep_y, turn_y, deep, n_h, s_h, n_deep, s_deep) = [
                    coef[index, kind, pl.ds(start, 8)] for index in range(COEFS - 1)
                ]
                slope = None if inner else coef[COEFS - 1, kind, pl.ds(start, 8)]
                for slot in slots:
                    u, u_n, u_s = (flow[group, source, slot, 0, r] for r in (here, up, down))
                    v, v_n, v_s = (flow[group, source, slot, 1, r] for r in (here, up, down))
                    h, h_n, h_s = (flow[group, source, slot, 2, r] for r in (here, up, down))
                    carried = deep * u
                    flow[group, target, slot, 0, here] = (
                        (keep_x * u + turn_x * v)
                        + (n * u_n + s * u_s)
                        + (roll(e * u - h, -1) + roll(w * u + h, 1))
                    )
                    flow[group, target, slot, 1, here] = (
                        (keep_y * v + turn_y * u)
                        + (n * v_n + s * v_s)
                        + (roll(e * v, -1) + roll(w * v, 1))
                        - (h_n - h_s if inner else slope * (h_n - h_s))
                    )
                    flow[group, target, slot, 2, here] = (
                        KEEP * h
                        + (roll(e_h * h - carried, -1) + roll(w_h * h + carried, 1))
                        + (n_h * h_n + s_h * h_s)
                        - (n_deep * v_n - s_deep * v_s)
                    )

    for to_east in (True, False):
        strip_copy(to_east, 0).wait_recv()
    for tile in (1, 2):
        place_base(tile)
    for start in (9, 15):
        rates(start)

    @pl.loop(0, GROUPS)
    def _(group):
        for tile in (1, 2):
            place_members(group, tile)
        for index, starts in enumerate(((9, 15), (10, 14), (11, 13), (12,))):
            advance(group, index % 2, 1 - index % 2, starts)

    for piece in ("wind", "height"):
        for north in (True, False):
            when_receives(north, lambda: lat_copies(piece, north).wait_recv())
    for to_east in (True, False):
        pl.when(has_south)(lambda: strip_copy(to_east, 1).wait_recv())
        pl.when(has_north)(lambda: strip_copy(to_east, -1).wait_recv())
    for tile in (0, 3):
        place_base(tile)
    for start in (1, 23):
        rates(start)

    @pl.loop(0, GROUPS)
    def _(group):
        for north in (True, False):
            when_receives(north, lambda: lat_copies(group, north).wait_recv())
        for tile in (0, 3):
            place_members(group, tile)

        rest = ((1, 23), (2, 22), (3, 21), (4, 20), (5, 12, 19), (6, 12, 18), (7, 12, 17), (8, 16))
        for index, starts in enumerate(rest):
            advance(group, index % 2, 1 - index % 2, starts)
        for local in range(GROUP):
            for var in range(3):
                for tile in range(2):
                    rows = pl.ds(8 + 8 * tile, 8)
                    main = flow[group, 0, local, var, rows]
                    side = roll(flow[group, 0, GROUP, var, rows], 128 - STRIP * (local + 1))
                    at = pl.multiple_of((group * GROUP + local) * 48 + var * 16 + tile * 8, 8)
                    evolved[pl.ds(at, 8), :] = (
                        jnp.where(lane8 < 128 - 2 * WIDTH, main, side) * (1.0 / PULL if var == 2 else 1.0)
                    )

    pl.semaphore_wait(level_known.at[0], 2)
    for step in (4, -4):
        pl.semaphore_signal(level_known.at[1], inc=1, device_id=level_peer(step))

    flat = jnp.concatenate([evolved[pl.ds(j, 16, stride=48), :] for j in range(48)], axis=1)
    gram = lax.dot_general(
        flat,
        flat,
        (((1,), (1,)), ((), ())),
        precision=lax.Precision.HIGHEST,
        preferred_element_type=jnp.float32,
    )
    table[0:16, :] = jnp.zeros((16, 128), jnp.float32)
    table[0:16, 0:16] = gram
    row_id, lane = rows_of(16), lane16
    wide = table[0:16, :]
    wide = wide + roll(jnp.where((lane >= 8) & (lane < 12), wide, 0.0), 4)
    for shift in (16, 32, 64):
        wide = wide + roll(wide, shift)
    upper = (row_id < 8) & (lane // 16 == row_id) & (lane % 16 < 12)
    lower = (row_id >= 8) & (row_id < 12) & (lane // 16 == row_id - 8) & (lane % 16 >= 12)
    pick = upper | lower
    packed = jnp.sum(jnp.where(pick, wide, 0.0), axis=0, keepdims=True)

    def exchange_copy(slot, step, place):
        buffer, peer_of, send, recv = (
            (plane_in, plane_peer, plane_send, plane_recv),
            (column_in, column_peer, column_send, column_recv),
        )[slot]
        return pltpu.make_async_remote_copy(
            src_ref=row_out.at[slot],
            dst_ref=buffer.at[place],
            send_sem=send,
            recv_sem=recv,
            device_id=peer_of(step),
        )

    def exchange_all(slot):
        buffer, peer_of, send, recv = (
            (plane_in, plane_peer, plane_send, plane_recv),
            (column_in, column_peer, column_send, column_recv),
        )[slot]
        rows = buffer.at[pl.ds(1, buffer.shape[0] - 1)]
        return pltpu.make_async_remote_copy(
            src_ref=rows, dst_ref=rows, send_sem=send, recv_sem=recv, device_id=peer_of(1)
        )

    def exchange(value, slot, buffer, me, order, beside):
        row_out[slot] = value
        buffer[me] = value
        for step in order:
            exchange_copy(slot, step, me).start()
        beside()
        exchange_all(slot).wait_recv()
        parts = [buffer[index] for index in range(len(order) + 1)]
        while len(parts) > 1:
            parts = [a + b for a, b in zip(parts[0::2], parts[1::2])]
        return parts[0]

    def halo_sent():
        for piece in ("wind", "height", 0, 1, 2):
            for north in (True, False):
                when_sends(north, lambda: lat_copies(piece, north).wait_send())
        for to_east in (True, False):
            strip_copy(to_east, 0).wait_send()
            pl.when(has_north)(lambda: strip_copy(to_east, 1).wait_send())
            pl.when(has_south)(lambda: strip_copy(to_east, -1).wait_send())

    def plane_sent():
        exchange_all(0).wait_send()

    def hops(step):
        pair = {0: 0, 1: 1, 2: 2, 3: 1}
        return pair[(step >> 1) & 3] + pair[(step >> 3) & 3]

    plane_order = sorted(range(1, n_plane), key=lambda step: -hops(step))
    column_order = sorted(range(1, n_level), key=lambda step: -min(step, n_level - step))

    pl.semaphore_wait(plane_known, 3)
    packed = exchange(packed, 0, plane_in, me_plane, plane_order, halo_sent)
    pl.semaphore_wait(level_known.at[1], 2)
    packed = exchange(packed, 1, column_in, level, column_order, plane_sent)

    row_ref[...] = packed
    exchange_all(1).wait_send()


def finish(cells, evolved, row_ref, fields_hbm, factor_hbm, table, out, factor_ref, sems):
    row_id, lane = rows_of(16), lanes_of(16)
    packed = row_ref[...]

    work = jnp.broadcast_to(packed / cells, (16, 128))
    for bit in range(3):
        work = jnp.where((row_id // (1 << bit)) % 2 == 1, roll(work, -(16 << bit)), work)
    work = jnp.where(row_id >= 8, roll(work, -4), work)
    turned = jnp.transpose(work)[0:16, :]
    table[0:16, 0:16] = turned
    turned = table[0:16, :]
    work = jnp.where((row_id >= 8) & (lane < 8), turned, work)
    work = jnp.where((lane < 12) & (row_id < 12), work, 0.0)
    left = [jnp.broadcast_to(work[:, k : k + 1], (16, 128)) for k in range(MEMBERS)]
    right = [jnp.where(row_id == k, 1.0, 0.0) for k in range(MEMBERS)]
    scales = []
    for k in range(MEMBERS):
        pivot = left[k][k : k + 1, :]
        scales.append(pivot)
        if k == MEMBERS - 1:
            break
        weight = jnp.where(row_id > k, left[k] * (1.0 / pivot), 0.0)
        for j in range(k + 1, MEMBERS):
            left[j] = left[j] - weight * left[j][k : k + 1, :]
        for j in range(k + 1):
            right[j] = right[j] - weight * right[j][k : k + 1, :]
    spread = jnp.ones((16, 128), jnp.float32)
    for k in range(MEMBERS):
        spread = jnp.where(row_id == k, scales[k], spread)
    spread = 1.0 / jnp.sqrt(spread)
    factor = jnp.zeros((16, 128), jnp.float32)
    for k in range(MEMBERS):
        factor = jnp.where((lane == k) & (row_id <= k), left[k], factor)
        table[16 * k : 16 * k + 16, :] = right[k] * spread
    factor_ref[...] = (factor * spread)[0:MEMBERS, 0:MEMBERS]
    factor_out = pltpu.make_async_copy(factor_ref, factor_hbm, sems.at[MEMBERS])
    factor_out.start()

    def copy_out(member):
        return pltpu.make_async_copy(out.at[member], fields_hbm.at[member], sems.at[member])

    for m in range(MEMBERS):
        scale = [jnp.broadcast_to(table[16 * k + m : 16 * k + m + 1, :], (8, 128)) for k in range(m + 1)]
        for place in range(6):
            total = None
            for k in range(m + 1):
                term = scale[k] * evolved[48 * k + 8 * place : 48 * k + 8 * place + 8, :]
                total = term if total is None else total + term
            out[m, place // 2, 8 * (place % 2) : 8 * (place % 2) + 8, :] = total
        copy_out(m).start()
    factor_out.wait()
    for m in range(MEMBERS):
        copy_out(m).wait()


def solution(mesh):
    n_lon, n_lat = mesh.shape["lon"], mesh.shape["lat"]
    n_plane, n_level = 2 * n_lat, n_lon // 2
    dma = pltpu.SemaphoreType.DMA

    def step(perturbations, base_wind, base_height):
        evolved, row = pl.pallas_call(
            functools.partial(kernel, n_lon, n_lat),
            out_shape=(
                pltpu.VMEM((16 * 48, 128), jnp.float32),
                pltpu.VMEM((1, 128), jnp.float32),
            ),
            in_specs=[pl.BlockSpec(memory_space=pl.ANY)] * 3,
            out_specs=(pl.BlockSpec(memory_space=pltpu.VMEM), pl.BlockSpec(memory_space=pltpu.VMEM)),
            scratch_shapes=[
                pltpu.VMEM((MEMBERS + 1, 3, 32, 128), jnp.float32),
                pltpu.VMEM((GROUPS, 16, 128), jnp.float32),
                pltpu.VMEM((GROUPS, 16, 128), jnp.float32),
                pltpu.VMEM((GROUPS, 32, 128), jnp.float32),
                pltpu.VMEM((GROUPS, 32, 128), jnp.float32),
                pltpu.VMEM((GROUPS, 2, GROUP + 1, 3, 32, 128), jnp.float32),
                pltpu.VMEM((2, 3, 32, 128), jnp.float32),
                pltpu.VMEM((COEFS, 2, 32, 128), jnp.float32),
                pltpu.VMEM((16, 128), jnp.float32),
                pltpu.VMEM((2, 1, 128), jnp.float32),
                pltpu.VMEM((n_plane, 1, 128), jnp.float32),
                pltpu.VMEM((n_level, 1, 128), jnp.float32),
                pltpu.VMEM((32, 128), jnp.float32),
                dma((3,)),
                dma((2, GROUPS + 2)),
                dma((2, GROUPS + 2)),
                dma((6,)),
                dma((6,)),
                dma,
                dma,
                dma,
                dma,
                pltpu.SemaphoreType.REGULAR,
                pltpu.SemaphoreType.REGULAR((2,)),
            ],
            compiler_params=pltpu.CompilerParams(collective_id=0, has_side_effects=True),
        )(perturbations, base_wind, base_height)
        return pl.pallas_call(
            functools.partial(finish, float(3 * 16 * n_lat * 128 * n_lon)),
            out_shape=(
                jax.ShapeDtypeStruct((MEMBERS, 3, 16, 128), jnp.float32),
                jax.ShapeDtypeStruct((MEMBERS, MEMBERS), jnp.float32),
            ),
            in_specs=[pl.BlockSpec(memory_space=pltpu.VMEM)] * 2,
            out_specs=(pl.BlockSpec(memory_space=pl.ANY), pl.BlockSpec(memory_space=pl.ANY)),
            scratch_shapes=[
                pltpu.VMEM((16 * MEMBERS, 128), jnp.float32),
                pltpu.VMEM((MEMBERS, 3, 16, 128), jnp.float32),
                pltpu.VMEM((MEMBERS, MEMBERS), jnp.float32),
                dma((MEMBERS + 1,)),
            ],
        )(
            pltpu.with_memory_space_constraint(evolved, pltpu.VMEM),
            pltpu.with_memory_space_constraint(row, pltpu.VMEM),
        )

    return jax.shard_map(
        step,
        mesh=mesh,
        in_specs=(P(None, None, "lat", "lon"), P(None, "lat", "lon"), P("lat", "lon")),
        out_specs=(P(None, None, "lat", "lon"), P()),
        check_vma=False,
    )
```
